32 devices in a mesh: ta: 2 (over core), ha: 2 (over x), wa: 8 (over z, y).
Axes of the slice: x: 2, y: 2, z: 4, core: 2. Of those that a mesh axis runs over, the one named last changes fastest.
Arguments:
- features: bfloat16 [2, 16, 28, 112, 1024], P(None, 'ta', 'ha', 'wa'), may hold values from -6 to 6
- teacher: bfloat16 [2, 16, 28, 112, 1000], P(None, 'ta', 'ha', 'wa'), may hold values from -30 to 750
- head_weight: float32 [1024, 1000], replicated, may hold values from -0.1875 to 0.1875
Outputs:
- feature_grad: bfloat16 [2, 16, 28, 112, 1024], P(None, 'ta', 'ha', 'wa')
- loss: float32 [], replicated
- new_weight: float32 [1024, 1000], P(('ta', 'ha', 'wa'))
The draws below stay inside these ranges and needn't reach their ends.
All inputs are finite; a program needn't handle non-finite values.
Results may differ from the reference program's by a relative error of at most 0.0056.
Values may be sent and summed in bfloat16 or wider, within the bound.
A program may use at most 192 MiB of HBM per device.

```python
import jax
import jax.numpy as jnp
from jax import lax

D = 1024
CLASSES = 1000
BATCH = 2
WW = 14
WV = 28
NT = 16
NH = 28
NW = 112


def draw_teacher(key, part):
    key_noise = jax.random.fold_in(jax.random.fold_in(key, 17), 0)
    shape = (BATCH, NT, NH, NW, CLASSES)
    return jnp.clip(3.0 * jax.random.normal(key_noise, shape, jnp.float32), -18.0, 18.0).astype(jnp.bfloat16)


def strengthened(array, own_key, source, target, parts, factor):
    owner, partner = [(jnp.arange(array.shape[axis_at]) // (array.shape[axis_at] // parts)).reshape([-1 if axis == axis_at else 1 for axis in range(array.ndim)]) for axis_at in (source, target)]
    chosen = jax.random.permutation(own_key, parts)[partner]
    strong = (owner == chosen) | (owner == (partner + parts // 2) % parts)
    return jnp.where(strong, factor * array, array)


def shard_levels(stream_key, extent, shards, least, top_value):
    loudness = 1.0
    for position, blocks in shards:
        draws = jax.random.uniform(jax.random.fold_in(jax.random.fold_in(stream_key, 6), position), (blocks,), jnp.float32, least / len(shards), top_value / len(shards))
        loudness = loudness * jnp.repeat(jnp.exp(draws), extent[position] // blocks).reshape((-1,) + (1,) * (len(extent) - 1 - position))
    return loudness


def centred(key, extent, spread, bound, shards=(), kind=jnp.bfloat16):
    factor_of = shard_levels(key, extent, shards, -0.22, 0.18) if shards else 1.0
    array = jax.random.normal(key, extent, jnp.float32) * spread * factor_of
    return jnp.minimum(jnp.maximum(array, -bound), bound).astype(kind)


def bell_draw_with(stream_key, dims, deviation, limit, pieces, heavy, kind=jnp.bfloat16):
    values = deviation * jax.random.normal(stream_key, dims, jnp.float32)
    if pieces:
        values = values * shard_levels(stream_key, dims, pieces, -0.22, 0.18)
    return jnp.clip(strengthened(values, jax.random.fold_in(stream_key, 3), *heavy), -limit, limit).astype(kind)


def setup_inputs(seed: int = 0) -> dict:
    keys = jax.random.split(jax.random.key(seed), 4)
    return {
        "features": bell_draw_with(keys[0], (BATCH, NT, NH, NW, D), 1.0, 6.0, ((1, 2), (2, 2), (3, 8)), (3, 4, 8, 2.0)),
        "teacher": draw_teacher(jax.random.fold_in(keys[3], 71), 0),
        "head_weight": centred(keys[2], (D, CLASSES), D ** -0.5, 0.1875, (), jnp.float32),
    }


sharpness_divisor = 2.0
learn_rate = 0.1
clip_norm = 1000.0

def pool_axis(values, reduce_dimension):
    width = [(0, 0)] * values.ndim
    width[reduce_dimension] = (1, 1)
    padded = jnp.pad(values, width)
    length = values.shape[reduce_dimension]
    first = lax.slice_in_dim(padded, 0, length, axis=reduce_dimension)
    middle = lax.slice_in_dim(padded, 1, length + 1, axis=reduce_dimension)
    last = lax.slice_in_dim(padded, 2, length + 2, axis=reduce_dimension)
    return first + middle + last

def clip_of(columns):
    return (columns + WV - WW // 2) // WV

def reference(features, teacher, head_weight):
    head_bf = head_weight.astype(jnp.bfloat16)
    blocks_wide = NW // WV
    teacher_padded = jnp.pad(teacher, ((0, 0), (0, 0), (0, 0), (1, 1), (0, 0)))
    frame_ids = jnp.arange(NT, dtype=jnp.int32)
    row_ids = jnp.arange(NH, dtype=jnp.int32)
    frame_count = (3.0 - (frame_ids == 0).astype(jnp.float32) - (frame_ids == NT - 1).astype(jnp.float32)).reshape(1, NT, 1, 1, 1)
    row_count = (3.0 - (row_ids == 0).astype(jnp.float32) - (row_ids == NH - 1).astype(jnp.float32)).reshape(1, 1, NH, 1, 1)

    def one_block(carry, block):
        head_grad, overall_objective, output = carry
        start = (block * WV).astype(jnp.int32)
        feat_block = lax.dynamic_slice_in_dim(features, start, WV, 3)
        teach_block = lax.dynamic_slice_in_dim(teacher_padded, start, WV + 2, 3).astype(jnp.float32)
        columns = start + jnp.arange(WV, dtype=jnp.int32)
        own_clip = clip_of(columns)
        left_ok = ((columns > 0) & (clip_of(columns - 1) == own_clip)).astype(jnp.float32).reshape(1, 1, 1, WV, 1)
        right_ok = ((columns < NW - 1) & (clip_of(columns + 1) == own_clip)).astype(jnp.float32).reshape(1, 1, 1, WV, 1)
        planar = pool_axis(pool_axis(teach_block, 1), 2)
        summed = planar[:, :, :, 0:WV] * left_ok + planar[:, :, :, 1:WV + 1] + planar[:, :, :, 2:WV + 2] * right_ok
        counts = frame_count * row_count * (1.0 + left_ok + right_ok)
        averaged_scores = (summed / counts).reshape(-1, CLASSES)
        feat_rows = feat_block.reshape(-1, D)
        pupil_scores = jnp.dot(feat_rows, head_bf, preferred_element_type=jnp.float32)
        pupil_entropy_terms = jax.nn.log_softmax(pupil_scores / sharpness_divisor, axis=-1)
        mentor_entropy_terms = jax.nn.log_softmax(averaged_scores / sharpness_divisor, axis=-1)
        mentor_likelihoods = jnp.exp(mentor_entropy_terms)
        pupil_likelihoods = jnp.exp(pupil_entropy_terms)
        patch_kullback_leibler = lax.optimization_barrier(jnp.sum(mentor_likelihoods * (mentor_entropy_terms - pupil_entropy_terms), axis=-1))
        overall_objective = overall_objective + sharpness_divisor * sharpness_divisor * jnp.sum(patch_kullback_leibler)
        score_slope = (sharpness_divisor * (pupil_likelihoods - mentor_likelihoods)).astype(jnp.bfloat16)
        feat_grad = lax.dot_general(score_slope, head_bf, (((1,), (1,)), ((), ())), preferred_element_type=jnp.float32)
        feat_grad = feat_grad.astype(jnp.bfloat16).reshape(feat_block.shape)
        output = lax.dynamic_update_slice_in_dim(output, feat_grad, start, 3)
        head_grad = head_grad + lax.dot_general(feat_rows, score_slope, (((0,), (0,)), ((), ())), preferred_element_type=jnp.float32)
        return ((head_grad, overall_objective, output), None)
    start_carry = (jnp.zeros((D, CLASSES), jnp.float32), jnp.zeros((), jnp.float32), jnp.zeros(features.shape, jnp.bfloat16))
    (head_grad, loss, feature_grad), _ = lax.scan(one_block, start_carry, jnp.arange(blocks_wide, dtype=jnp.int32))
    grad_norm = jnp.sqrt(jnp.sum(head_grad * head_grad))
    clip = jnp.minimum(1.0, clip_norm / (grad_norm + 1e-06))
    new_weight = head_weight - learn_rate * clip * head_grad
    return (feature_grad, loss, new_weight)
```

```python
import functools
import math

import jax
import jax.numpy as jnp
from jax import lax
from jax.experimental import pallas as pl
from jax.experimental.pallas import tpu as pltpu
from jax.sharding import PartitionSpec as P

WW = 14
WV = 28
AXES = ("ta", "ha", "wa")
MESH = pl.DeviceIdType.MESH

sharpness_divisor = 2.0
learn_rate = 0.1
clip_norm = 1000.0
EXP2_SCALE = math.log2(math.e) / sharpness_divisor

RING = 4
GROUP = 16
HEAD_CHUNK = 256


def step_kernel(n, teacher, feats, weight, fgrad, loss, new_weight, cells, features, logits, slopes, head, planar, partner, edge_sum,
                pool, inverse, part, final, own_rows, total, stat, stat_in, stat_out, stat_in2, landed, load_sem, feat_sem, col_send, col_recv, row_send,
                row_recv, edge_send, edge_recv, red_send, red_recv, stat_send, stat_recv, out_sem):
    batch, rows, columns, frames, classes = teacher.shape
    tokens, width = feats.shape
    ta, ha, wa = (lax.axis_index(axis) for axis in AXES)
    per_row = columns * frames
    slots = columns + 2
    sides = slots * frames
    outs = batch * per_row
    edges = batch * slots
    bits = n.bit_length() - 1
    owned = own_rows.shape[0]
    has_left, has_right = wa > 0, wa < n - 1

    barrier = pltpu.get_barrier_semaphore()

    def greet(device):
        pl.semaphore_signal(barrier, inc=1, device_id=device, device_id_type=MESH)

    @pl.loop(1, n)
    def _(k):
        greet({"wa": lax.rem(wa + k, n)})

    greet({"ta": 1 - ta})
    greet({"ha": 1 - ha})
    greet({"ta": 1 - ta, "ha": 1 - ha})

    @pl.when(has_left)
    def _():
        greet({"ha": 1 - ha, "wa": wa - 1})

    @pl.when(has_right)
    def _():
        greet({"ha": 1 - ha, "wa": wa + 1})

    staged = logits.at[pl.ds(0, width)]
    head_load = pltpu.make_async_copy(weight, staged, load_sem.at[0])
    head_load.start()
    fchunks = feat_sem.shape[0]
    chunk = tokens // fchunks

    def feat_rows(i):
        return pl.ds(pl.multiple_of(i * chunk, 16), chunk)

    def feat_load(i):
        return pltpu.make_async_copy(feats.at[feat_rows(i)], features.at[feat_rows(i)], feat_sem.at[i])

    @pl.loop(0, fchunks)
    def _(i):
        feat_load(i).start()

    cell_load = pltpu.make_async_copy(teacher, cells.at[:, pl.ds(0, rows), pl.ds(0, columns)], load_sem.at[1])
    cell_load.start()
    mine = (ta * 2 + ha) * n + wa
    own_load = pltpu.make_async_copy(weight.at[pl.ds(pl.multiple_of(mine * owned, owned), owned)], own_rows, load_sem.at[2])
    own_load.start()

    pl.semaphore_wait(barrier, n + 2 + has_left.astype(jnp.int32) + has_right.astype(jnp.int32))

    col_chunks = col_send.shape[1]
    span = rows // col_chunks

    def col_copy(side, q):
        start = jnp.where(ha == 0, q * span, rows - (q + 1) * span)
        at = pl.ds(start, span)
        return pltpu.make_async_remote_copy(
            src_ref=teacher.at[:, at, columns - 1 if side == 0 else 0], dst_ref=cells.at[:, at, columns + side],
            send_sem=col_send.at[side, q], recv_sem=col_recv.at[side, q],
            device_id={"wa": wa + 1 if side == 0 else wa - 1}, device_id_type=MESH)

    facing = jnp.where(ha == 0, rows - 1, 0)

    def row_copy():
        return pltpu.make_async_remote_copy(
            src_ref=teacher.at[:, facing], dst_ref=cells.at[:, rows, pl.ds(0, columns)], send_sem=row_send.at[2], recv_sem=row_recv.at[2],
            device_id={"ha": 1 - ha}, device_id_type=MESH)

    def corner_copy(side):
        return pltpu.make_async_remote_copy(
            src_ref=teacher.at[:, facing, columns - 1 if side == 0 else 0], dst_ref=cells.at[:, rows, columns + side],
            send_sem=row_send.at[side], recv_sem=row_recv.at[side],
            device_id={"ha": 1 - ha, "wa": wa + 1 if side == 0 else wa - 1}, device_id_type=MESH)

    sends = (has_right, has_left)
    gets = (has_left, has_right)

    @pl.loop(0, col_chunks)
    def _(q):
        for side in (0, 1):
            @pl.when(sends[side])
            def _():
                col_copy(side, q).start()

    row_copy().start()
    for side in (0, 1):
        @pl.when(sends[side])
        def _():
            corner_copy(side).start()

    base = lax.rem(wa * columns + WV - WW // 2, WV)

    def clip_at(col):
        at = col + base
        return jnp.where(at < 0, -1, jnp.where(at >= WV, 1, 0))

    grid_wide = columns * n
    out = lax.broadcasted_iota(jnp.int32, pool.shape, 0)
    src = lax.broadcasted_iota(jnp.int32, pool.shape, 1)
    is_edge = out >= outs
    edge_at = out - outs
    main_batch = (out >= per_row).astype(jnp.int32)
    edge_batch = (edge_at >= slots).astype(jnp.int32)
    out_batch = jnp.where(is_edge, edge_batch, main_batch)
    main_in = out - main_batch * per_row
    out_col = jnp.where(is_edge, edge_at - edge_batch * slots, main_in // frames)
    out_frame = lax.rem(main_in, frames)
    src_batch = (src >= sides).astype(jnp.int32)
    src_in = src - src_batch * sides
    src_slot = src_in // frames
    src_frame = lax.rem(src_in, frames)
    src_col = jnp.where(src_slot == columns, -1, jnp.where(src_slot == columns + 1, columns, src_slot))
    edge_frame = jnp.where(ta == 0, frames - 1, 0)
    src_at = src_col + wa * columns
    away = jnp.where(is_edge, src_frame - edge_frame, src_frame - out_frame)
    reach = jnp.where(is_edge, 0, 1)
    taken = (
        (out_batch == src_batch) & (out_col < columns) & (jnp.abs(out_col - src_col) <= 1) & (jnp.abs(away) <= reach)
        & (src_at >= 0) & (src_at < grid_wide) & (clip_at(out_col) == clip_at(src_col))
    )
    pool[...] = jnp.where(taken, 1.0, 0.0).astype(jnp.bfloat16)
    cell = lax.broadcasted_iota(jnp.int32, inverse.shape, 0)
    col, frame = cell // frames, lax.rem(cell, frames)
    at = col + wa * columns
    left_ok = (at > 0) & (clip_at(col - 1) == clip_at(col))
    right_ok = (at < grid_wide - 1) & (clip_at(col + 1) == clip_at(col))
    frame_at = frame + ta * frames
    frame_edge = (frame_at == 0) | (frame_at == 2 * frames - 1)
    cols = 1.0 + jnp.where(left_ok, 1.0, 0.0) + jnp.where(right_ok, 1.0, 0.0)
    inverse[...] = EXP2_SCALE / (cols * jnp.where(frame_edge, 2.0, 3.0))

    for side in (0, 1):
        @pl.when(jnp.logical_not(gets[side]))
        def _():
            cells[:, :, columns + side] = jnp.zeros((batch, rows + 1, frames, classes), cells.dtype)

    planar[0] = jnp.zeros(planar.shape[1:], jnp.float32)
    partner[0] = jnp.zeros(partner.shape[1:], jnp.float32)

    padded = head.shape[1]
    tail = classes // 128 * 128
    head[:, pl.ds(tail, padded - tail)] = jnp.zeros((width, padded - tail), jnp.bfloat16)
    head_load.wait()

    @pl.loop(0, width // 128)
    def _(i):
        at = pl.ds(pl.multiple_of(i * 128, 128), 128)
        head[at, pl.ds(0, classes)] = logits[at].astype(jnp.bfloat16)

    def student_rows(start):
        at = pl.ds(pl.multiple_of(start, GROUP), GROUP)
        value = logits[at] * EXP2_SCALE
        value = value - jnp.max(value, -1, keepdims=True)
        norm = jnp.log2(jnp.sum(jnp.exp2(value), -1, keepdims=True))
        logits[at] = value - norm

    @pl.loop(0, fchunks)
    def _(i):
        feat_load(i).wait()
        logits[feat_rows(i)] = jnp.dot(features[feat_rows(i)], head[:, pl.ds(0, classes)], preferred_element_type=jnp.float32)
        slopes[feat_rows(i), pl.ds(tail, padded - tail)] = jnp.zeros((chunk, padded - tail), jnp.bfloat16)

        @pl.loop(0, chunk // GROUP, unroll=4)
        def _(g):
            student_rows(i * chunk + g * GROUP)

    cell_load.wait()
    total[...] = jnp.zeros_like(total)

    def row_of(k):
        return jnp.where(k > rows, rows, jnp.where(ha == 0, k - 1, rows - k))

    def edge_copy(k):
        return pltpu.make_async_remote_copy(
            src_ref=planar.at[lax.rem(k, RING), pl.ds(outs, edges)], dst_ref=partner.at[k],
            send_sem=edge_send.at[lax.rem(k, RING)], recv_sem=edge_recv.at[k], device_id={"ta": 1 - ta}, device_id_type=MESH)

    @pl.loop(1, rows + 3)
    def _(it):
        @pl.when(it <= rows + 1)
        def _():
            @pl.when((it <= rows) & (lax.rem(it - 1, span) == 0))
            def _():
                for side in (0, 1):
                    @pl.when(gets[side])
                    def _():
                        col_copy(side, (it - 1) // span).wait_recv()

            @pl.when(it == rows + 1)
            def _():
                row_copy().wait_recv()
                for side in (0, 1):
                    @pl.when(gets[side])
                    def _():
                        corner_copy(side).wait_recv()

            @pl.when(it > RING)
            def _():
                edge_copy(it - RING).wait_send()

            here = cells[:, row_of(it)].reshape(batch * sides, classes)
            planar[lax.rem(it, RING)] = jnp.dot(pool[...], here, preferred_element_type=jnp.float32)
            edge_copy(it).start()

        @pl.when(it > 1)
        def _():
            edge_copy(it - 1).wait_recv()

        @pl.when(it > 2)
        def _():
            k = it - 2
            row = row_of(k)
            edge_sum[...] = partner[k - 1] + partner[k] + partner[k + 1]
            row_at = row + ha * rows
            row_scale = jnp.where((row_at == 0) | (row_at == 2 * rows - 1), 1.0 / 2.0, 1.0 / 3.0)
            before, now, after = (lax.rem(k + RING - 1, RING), lax.rem(k, RING), lax.rem(k + 1, RING))
            frame_in = lax.rem(lax.broadcasted_iota(jnp.int32, (GROUP, 1), 0), frames)
            take = jnp.where(frame_in == jnp.where(ta == 0, frames - 1, 0), 1.0, 0.0)
            per_group = GROUP // frames

            @pl.loop(0, batch * per_row // GROUP, unroll=2)
            def _(g):
                b = (g >= per_row // GROUP).astype(jnp.int32)
                in_row = g - b * (per_row // GROUP)
                sl = pl.ds(pl.multiple_of(g * GROUP, GROUP), GROUP)
                pooled = planar[before, sl] + planar[now, sl] + planar[after, sl]
                extra = [jnp.broadcast_to(edge_sum[pl.ds(b * slots + in_row * per_group + i, 1)], (frames, classes)) for i in range(per_group)]
                pooled = pooled + take * jnp.concatenate(extra, 0)
                scale = inverse[pl.ds(pl.multiple_of(in_row * GROUP, GROUP), GROUP), pl.ds(0, 1)] * row_scale
                teach = pooled * scale
                teach = teach - jnp.max(teach, -1, keepdims=True)
                power = jnp.exp2(teach)
                norm = jnp.sum(power, -1, keepdims=True)
                at = pl.ds(pl.multiple_of(b * (rows * per_row) + row * per_row + in_row * GROUP, GROUP), GROUP)
                learn = logits[at]
                cross = jnp.sum(power * (teach - learn), -1, keepdims=True)
                total[...] += cross / norm - jnp.log2(norm)
                slope = jnp.exp2(learn + 1.0) - power * (2.0 / norm)
                slopes[at, pl.ds(0, classes)] = slope.astype(jnp.bfloat16)

    @pl.loop(rows + 2 - RING, rows + 2)
    def _(k):
        edge_copy(k).wait_send()

    dims = 2 + bits
    my_bits = [ta, ha] + [lax.rem(wa // (1 << (bits - 1 - i)), 2) for i in range(bits)]
    chunks = padded // HEAD_CHUNK
    near = 2 + bits - 1

    def order(j):
        first = [1, near] if j % 2 == 0 else [near, 1]
        return [0] + first + [2 + i for i in reversed(range(bits - 1))]

    def partner_of(d):
        if d == 0:
            return {"ta": 1 - ta}
        if d == 1:
            return {"ha": 1 - ha}
        return {"wa": wa + (1 - 2 * my_bits[d]) * (1 << (bits - 1 - (d - 2)))}

    def region(j, s, other):
        seq = order(j)
        index = [slice(None)] * dims
        for d in seq[:s]:
            index[d] = my_bits[d]
        index[seq[s]] = 1 - my_bits[seq[s]] if other else my_bits[seq[s]]
        return (j, *index)

    def red_copy(j, s):
        return pltpu.make_async_remote_copy(
            src_ref=part.at[region(j, s, True)], dst_ref=landed[s].at[j], send_sem=red_send.at[j, s], recv_sem=red_recv.at[j, s],
            device_id=partner_of(order(j)[s]), device_id_type=MESH)

    def head_grad(j):
        half = width // 2
        parts = []
        for h in range(2):
            grad = lax.dot_general(features[:, pl.ds(h * half, half)], slopes[:, pl.ds(j * HEAD_CHUNK, HEAD_CHUNK)],
                                   (((0,), (0,)), ((), ())), preferred_element_type=jnp.float32)
            part[j, h] = grad.astype(part.dtype).reshape(part.shape[2:])
        red_copy(j, 0).start()

    def advance(j, s):
        red_copy(j, s).wait_recv()
        value = part[region(j, s, False)].astype(jnp.float32) + landed[s][j].astype(jnp.float32)
        if s + 1 < dims:
            part[region(j, s, False)] = value.astype(part.dtype)
            red_copy(j, s + 1).start()
        else:
            final[:, pl.ds(j * HEAD_CHUNK, HEAD_CHUNK)] = value

    def out_copy(i):
        return pltpu.make_async_copy(features.at[feat_rows(i)], fgrad.at[feat_rows(i)], out_sem.at[i])

    def feature_grad(i):
        grad = lax.dot_general(slopes[feat_rows(i)], head[...], (((1,), (1,)), ((), ())), preferred_element_type=jnp.float32)
        features[feat_rows(i)] = grad.astype(features.dtype)
        out_copy(i).start()

    waits = [1.5, 3.2, 2.0] + [1.4] * (dims - 3)
    events = []
    for j in range(chunks):
        ready = 2.3 * (j + 1)
        for s in range(dims):
            ready += waits[s]
            events.append((ready, j, s))
    events.sort()
    clock = 0.0
    for op in [(head_grad, j, 2.3) for j in range(chunks)] + [(feature_grad, i, 1.2) for i in range(fchunks)]:
        op[0](op[1])
        clock += op[2]
        while events and events[0][0] <= clock:
            _, j, s = events.pop(0)
            advance(j, s)
    for _, j, s in events:
        advance(j, s)

    grad = final[...]
    squares = jnp.sum(jnp.sum(grad * grad, axis=1, keepdims=True), axis=0, keepdims=True)
    spent = jnp.sum(total[...], axis=0, keepdims=True) * (sharpness_divisor * sharpness_divisor * math.log(2.0))
    lane = lax.broadcasted_iota(jnp.int32, stat.shape, 1)
    stat[...] = jnp.where(lane == 0, squares, jnp.where(lane == 1, spent, 0.0))

    def stat_copy(k):
        return pltpu.make_async_remote_copy(
            src_ref=stat, dst_ref=stat_in.at[k], send_sem=stat_send.at[k], recv_sem=stat_recv.at[k],
            device_id={"wa": lax.rem(wa + k, n)}, device_id_type=MESH)

    @pl.loop(1, n)
    def _(k):
        stat_copy(k).start()

    stat_in[0] = stat[...]

    @pl.loop(1, n)
    def _(k):
        stat_copy(k).wait_recv()

    stat_out[...] = jnp.sum(stat_in[...], axis=0)
    others = ({"ta": 1 - ta}, {"ha": 1 - ha}, {"ta": 1 - ta, "ha": 1 - ha})
    second = [
        pltpu.make_async_remote_copy(
            src_ref=stat_out, dst_ref=stat_in2.at[k], send_sem=stat_send.at[n + k], recv_sem=stat_recv.at[n + k],
            device_id=device, device_id_type=MESH)
        for k, device in enumerate(others)
    ]
    for copy in second:
        copy.start()
    for copy in second:
        copy.wait_recv()
    lows = [stat_out[...]] + [stat_in2[k] for k in range(3)]
    both = (lows[0] + lows[1]) + (lows[2] + lows[3])
    norm = jnp.sqrt(both[0:1, 0:1])
    loss[...] = both[0:1, 1:2]
    clip = jnp.minimum(1.0, clip_norm / (norm + 1e-06))
    own_load.wait()
    new_weight[...] = own_rows[...] - learn_rate * clip * final[:, pl.ds(0, classes)]

    for copy in second:
        copy.wait_send()

    @pl.loop(1, n)
    def _(k):
        stat_copy(k).wait_send()

    for j in range(chunks):
        for s in range(dims):
            red_copy(j, s).wait_send()

    @pl.loop(0, fchunks)
    def _(i):
        out_copy(i).wait()

    row_copy().wait_send()
    for side in (0, 1):
        @pl.when(sends[side])
        def _():
            corner_copy(side).wait_send()

            @pl.loop(0, col_chunks)
            def _(q):
                col_copy(side, q).wait_send()


def local(features, teacher, head_weight):
    features, teacher = (jnp.transpose(array, (0, 2, 3, 1, 4)) for array in (features, teacher))
    batch, rows, columns, frames, width = features.shape
    classes = teacher.shape[-1]
    tokens = batch * rows * columns * frames
    n = lax.axis_size("wa")
    bits = n.bit_length() - 1
    devices = 4 * n
    owned = width // devices
    padded = -(-classes // HEAD_CHUNK) * HEAD_CHUNK
    chunks = padded // HEAD_CHUNK
    dims = 2 + bits
    outs = batch * columns * frames
    edges = batch * (columns + 2)
    fchunks = rows // 2
    col_chunks = rows // 2
    f32, bf16 = jnp.float32, jnp.bfloat16
    dma = pltpu.SemaphoreType.DMA
    any_space = pl.BlockSpec(memory_space=pl.ANY)
    vmem = pl.BlockSpec(memory_space=pltpu.VMEM)
    fgrad, loss, new_weight = pl.pallas_call(
        functools.partial(step_kernel, n),
        in_specs=[any_space] * 3,
        out_specs=[any_space, vmem, vmem],
        out_shape=[
            jax.ShapeDtypeStruct((tokens, width), features.dtype),
            jax.ShapeDtypeStruct((1, 1), f32),
            jax.ShapeDtypeStruct((owned, classes), f32),
        ],
        scratch_shapes=[
            pltpu.VMEM((batch, rows + 1, columns + 2, frames, classes), bf16),
            pltpu.VMEM((tokens, width), bf16),
            pltpu.VMEM((tokens, classes), f32),
            pltpu.VMEM((tokens, padded), bf16),
            pltpu.VMEM((width, padded), bf16),
            pltpu.VMEM((RING, outs + edges, classes), f32),
            pltpu.VMEM((rows + 2, edges, classes), f32),
            pltpu.VMEM((edges, classes), f32),
            pltpu.VMEM((outs + edges, batch * (columns + 2) * frames), bf16),
            pltpu.VMEM((columns * frames, 128), f32),
            pltpu.VMEM((chunks, 2, 2) + (2,) * bits + (owned, HEAD_CHUNK), bf16),
            pltpu.VMEM((owned, padded), f32),
            pltpu.VMEM((owned, classes), f32),
            pltpu.VMEM((GROUP, 1), f32),
            pltpu.VMEM((8, 128), f32),
            pltpu.VMEM((n, 8, 128), f32),
            pltpu.VMEM((8, 128), f32),
            pltpu.VMEM((3, 8, 128), f32),
            [pltpu.VMEM((chunks,) + (2,) * (dims - 1 - s) + (owned, HEAD_CHUNK), bf16) for s in range(dims)],
            dma((3,)),
            dma((fchunks,)),
            dma((2, col_chunks)),
            dma((2, col_chunks)),
            dma((3,)),
            dma((3,)),
            dma((RING,)),
            dma((rows + 2,)),
            dma((chunks, dims)),
            dma((chunks, dims)),
            dma((n + 3,)),
            dma((n + 3,)),
            dma((fchunks,)),
        ],
        compiler_params=pltpu.CompilerParams(collective_id=0, has_side_effects=True, vmem_limit_bytes=63 * 1024 * 1024),
    )(teacher, features.reshape(tokens, width), head_weight)
    fgrad = jnp.transpose(fgrad.reshape(features.shape), (0, 3, 1, 2, 4))
    return fgrad, loss[0, 0], new_weight


def solution(mesh):
    assert mesh.shape["ta"] == 2 and mesh.shape["ha"] == 2
    placed = (P(None, "ta", "ha", "wa", None), P(None, "ta", "ha", "wa", None), P())
    return jax.shard_map(
        local,
        mesh=mesh,
        in_specs=placed,
        out_specs=(P(None, "ta", "ha", "wa", None), P(), P(AXES, None)),
        check_vma=False,
    )
```

```python
import functools
import math

import jax
import jax.numpy as jnp
from jax import lax
from jax.experimental import pallas as pl
from jax.experimental.pallas import tpu as pltpu
from jax.sharding import PartitionSpec as P

WW = 14
WV = 28
AXES = ("ta", "ha", "wa")
MESH = pl.DeviceIdType.MESH

sharpness_divisor = 2.0
learn_rate = 0.1
clip_norm = 1000.0
EXP2_SCALE = math.log2(math.e) / sharpness_divisor

RING = 4
GROUP = 16
HEAD_CHUNK = 256
LANES = 128
LOW = -1e30


def step_kernel(n, teacher, feats, weight, fgrad, loss, new_weight, cells, features, logits, slopes, head, planar, partner, peak, shift,
                pool, inverse, part, final, own_rows, own_turned, total, stat, stat_in, stat_out, stat_in2, landed, load_sem, feat_sem, col_send, col_recv, row_send,
                row_recv, edge_send, edge_recv, red_send, red_recv, stat_send, stat_recv, out_sem):
    batch, rows, columns, frames, classes = teacher.shape
    tokens, width = feats.shape
    ta, ha, wa = (lax.axis_index(axis) for axis in AXES)
    per_row = columns * frames
    slots = columns + 2
    sides = slots * frames
    outs = batch * per_row
    edges = planar.shape[2] - outs
    bits = n.bit_length() - 1
    owned = final.shape[0]
    has_left, has_right = wa > 0, wa < n - 1

    barrier = pltpu.get_barrier_semaphore()

    def greet(device):
        pl.semaphore_signal(barrier, inc=1, device_id=device, device_id_type=MESH)

    @pl.loop(1, n)
    def _(k):
        greet({"wa": lax.rem(wa + k, n)})

    greet({"ta": 1 - ta})
    greet({"ha": 1 - ha})
    greet({"ta": 1 - ta, "ha": 1 - ha})

    @pl.when(has_left)
    def _():
        greet({"ha": 1 - ha, "wa": wa - 1})

    @pl.when(has_right)
    def _():
        greet({"ha": 1 - ha, "wa": wa + 1})

    staged = logits.at[pl.ds(0, classes)]
    head_load = pltpu.make_async_copy(weight, staged, load_sem.at[0])
    head_load.start()
    fchunks = feat_sem.shape[0]
    chunk = tokens // fchunks

    def feat_rows(i):
        return pl.ds(pl.multiple_of(i * chunk, 16), chunk)

    def feat_load(i):
        return pltpu.make_async_copy(feats.at[feat_rows(i)], features.at[feat_rows(i)], feat_sem.at[i])

    @pl.loop(0, fchunks)
    def _(i):
        feat_load(i).start()

    cell_load = pltpu.make_async_copy(teacher, cells.at[:, pl.ds(0, rows), pl.ds(0, columns)], load_sem.at[1])
    cell_load.start()
    mine = (ta * 2 + ha) * n + wa
    first_row = mine * owned
    lane_block = pl.ds(pl.multiple_of(first_row // LANES * LANES, LANES), LANES)
    own_load = pltpu.make_async_copy(weight.at[:, lane_block], own_rows, load_sem.at[2])
    own_load.start()

    pl.semaphore_wait(barrier, n + 2 + has_left.astype(jnp.int32) + has_right.astype(jnp.int32))

    col_chunks = col_send.shape[1]
    span = rows // col_chunks

    def col_copy(side, q):
        start = jnp.where(ha == 0, q * span, rows - (q + 1) * span)
        at = pl.ds(start, span)
        return pltpu.make_async_remote_copy(
            src_ref=teacher.at[:, at, columns - 1 if side == 0 else 0], dst_ref=cells.at[:, at, columns + side],
            send_sem=col_send.at[side, q], recv_sem=col_recv.at[side, q],
            device_id={"wa": wa + 1 if side == 0 else wa - 1}, device_id_type=MESH)

    facing = jnp.where(ha == 0, rows - 1, 0)

    def row_copy():
        return pltpu.make_async_remote_copy(
            src_ref=teacher.at[:, facing], dst_ref=cells.at[:, rows, pl.ds(0, columns)], send_sem=row_send.at[2], recv_sem=row_recv.at[2],
            device_id={"ha": 1 - ha}, device_id_type=MESH)

    def corner_copy(side):
        return pltpu.make_async_remote_copy(
            src_ref=teacher.at[:, facing, columns - 1 if side == 0 else 0], dst_ref=cells.at[:, rows, columns + side],
            send_sem=row_send.at[side], recv_sem=row_recv.at[side],
            device_id={"ha": 1 - ha, "wa": wa + 1 if side == 0 else wa - 1}, device_id_type=MESH)

    sends = (has_right, has_left)
    gets = (has_left, has_right)

    @pl.loop(0, col_chunks)
    def _(q):
        for side in (0, 1):
            @pl.when(sends[side])
            def _():
                col_copy(side, q).start()

    row_copy().start()
    for side in (0, 1):
        @pl.when(sends[side])
        def _():
            corner_copy(side).start()

    base = lax.rem(wa * columns + WV - WW // 2, WV)

    def clip_at(col):
        at = col + base
        return jnp.where(at < 0, -1, jnp.where(at >= WV, 1, 0))

    grid_wide = columns * n
    out = lax.broadcasted_iota(jnp.int32, pool.shape, 0)
    src = lax.broadcasted_iota(jnp.int32, pool.shape, 1)
    is_edge = out >= outs
    edge_at = out - outs
    main_batch = (out >= per_row).astype(jnp.int32)
    edge_batch = (edge_at >= columns).astype(jnp.int32)
    out_batch = jnp.where(is_edge, edge_batch, main_batch)
    main_in = out - main_batch * per_row
    out_col = jnp.where(is_edge, edge_at - edge_batch * columns, main_in // frames)
    out_frame = lax.rem(main_in, frames)
    src_batch = (src >= sides).astype(jnp.int32)
    src_in = src - src_batch * sides
    src_slot = src_in // frames
    src_frame = lax.rem(src_in, frames)
    src_col = jnp.where(src_slot == columns, -1, jnp.where(src_slot == columns + 1, columns, src_slot))
    edge_frame = jnp.where(ta == 0, frames - 1, 0)
    src_at = src_col + wa * columns
    away = jnp.where(is_edge, src_frame - edge_frame, src_frame - out_frame)
    reach = jnp.where(is_edge, 0, 1)
    taken = (
        (out_batch == src_batch) & (out_col < columns) & (jnp.abs(out_col - src_col) <= 1) & (jnp.abs(away) <= reach)
        & (src_at >= 0) & (src_at < grid_wide) & (clip_at(out_col) == clip_at(src_col))
    )
    pool[...] = jnp.where(taken, 1.0, 0.0).astype(jnp.bfloat16)
    cell = lax.broadcasted_iota(jnp.int32, inverse.shape, 0)
    col, frame = cell // frames, lax.rem(cell, frames)
    at = col + wa * columns
    left_ok = (at > 0) & (clip_at(col - 1) == clip_at(col))
    right_ok = (at < grid_wide - 1) & (clip_at(col + 1) == clip_at(col))
    frame_at = frame + ta * frames
    frame_edge = (frame_at == 0) | (frame_at == 2 * frames - 1)
    cols = 1.0 + jnp.where(left_ok, 1.0, 0.0) + jnp.where(right_ok, 1.0, 0.0)
    inverse[...] = EXP2_SCALE / (cols * jnp.where(frame_edge, 2.0, 3.0))

    for side in (0, 1):
        @pl.when(jnp.logical_not(gets[side]))
        def _():
            cells[:, :, columns + side] = jnp.zeros((batch, rows + 1, frames, classes), cells.dtype)

    planar[0] = jnp.zeros(planar.shape[1:], jnp.float32)

    padded = head.shape[0]
    blocks = padded // LANES
    head_load.wait()

    @pl.loop(0, blocks)
    def _(i):
        at = pl.ds(pl.multiple_of(i * LANES, LANES), LANES)
        class_at = lax.broadcasted_iota(jnp.int32, (LANES, 1), 0) + i * LANES
        head[at] = jnp.where(class_at < classes, logits[at], 0.0).astype(jnp.bfloat16)

    own_load.wait()
    own_turned[...] = own_rows[...].T

    lane_at = lax.broadcasted_iota(jnp.int32, (GROUP, LANES), 1)
    real = lane_at < classes - (blocks - 1) * LANES

    def lanes(j):
        return pl.ds(j * LANES, LANES)

    def fold(values, op):
        values = list(values)
        while len(values) > 1:
            values = [op(*values[i : i + 2]) if i + 1 < len(values) else values[i] for i in range(0, len(values), 2)]
        return values[0]

    def masked(values):
        return values[:-1] + [jnp.where(real, values[-1], LOW)]

    @pl.loop(0, fchunks)
    def _(i):
        feat_load(i).wait()
        logits[feat_rows(i)] = lax.dot_general(features[feat_rows(i)], head[...], (((1,), (1,)), ((), ())), preferred_element_type=jnp.float32)

        @pl.loop(0, chunk // GROUP, unroll=7)
        def _(g):
            at = pl.ds(pl.multiple_of(i * chunk + g * GROUP, GROUP), GROUP)
            top = jnp.max(fold(masked([logits[at, lanes(j)] for j in range(blocks)]), jnp.maximum), -1, keepdims=True)
            peak[pl.ds(pl.multiple_of(g * GROUP, GROUP), GROUP)] = jnp.broadcast_to(top * EXP2_SCALE, (GROUP, LANES))

        @pl.loop(0, chunk // GROUP, unroll=7)
        def _(g):
            at = pl.ds(pl.multiple_of(i * chunk + g * GROUP, GROUP), GROUP)
            high = peak[pl.ds(pl.multiple_of(g * GROUP, GROUP), GROUP)]
            powers = [jnp.exp2(value * EXP2_SCALE - high) for value in masked([logits[at, lanes(j)] for j in range(blocks)])]
            norm = jnp.sum(fold(powers, jnp.add), -1, keepdims=True)
            shift[at] = high + jnp.log2(norm)

    cell_load.wait()
    total[...] = jnp.zeros_like(total)

    def row_of(k):
        return jnp.where(k > rows, rows, jnp.where(ha == 0, k - 1, rows - k))

    def edge_copy(k):
        return pltpu.make_async_remote_copy(
            src_ref=planar.at[lax.rem(k, RING), :, pl.ds(outs, edges)], dst_ref=partner.at[k],
            send_sem=edge_send.at[lax.rem(k, RING)], recv_sem=edge_recv.at[k], device_id={"ta": 1 - ta}, device_id_type=MESH)

    @pl.loop(1, rows + 3)
    def _(it):
        @pl.when(it <= rows + 1)
        def _():
            @pl.when((it <= rows) & (lax.rem(it - 1, span) == 0))
            def _():
                for side in (0, 1):
                    @pl.when(gets[side])
                    def _():
                        col_copy(side, (it - 1) // span).wait_recv()

            @pl.when(it == rows + 1)
            def _():
                row_copy().wait_recv()
                for side in (0, 1):
                    @pl.when(gets[side])
                    def _():
                        corner_copy(side).wait_recv()

            @pl.when(it > RING)
            def _():
                edge_copy(it - RING).wait_send()

            here = cells[:, row_of(it)].reshape(batch * sides, classes)
            sums = jnp.dot(pool[...], here, preferred_element_type=jnp.float32)
            for j in range(blocks):
                wide = min(LANES, classes - j * LANES)
                planar[lax.rem(it, RING), j, :, pl.ds(0, wide)] = sums[:, j * LANES : j * LANES + wide]
            edge_copy(it).start()

        @pl.when(it > 1)
        def _():
            edge_copy(it - 1).wait_recv()
            slot = lax.rem(it - 1, RING)
            at = pl.ds(jnp.where(ta == 0, frames - 1, 0), batch * columns, stride=frames)
            for j in range(blocks):
                planar[slot, j, at] += partner[it - 1, j, pl.ds(0, batch * columns)]

        @pl.when(it > 2)
        def _():
            k = it - 2
            row = row_of(k)
            row_at = row + ha * rows
            row_scale = jnp.where((row_at == 0) | (row_at == 2 * rows - 1), 1.0 / 2.0, 1.0 / 3.0)
            before, now, after = (lax.rem(k + RING - 1, RING), lax.rem(k, RING), lax.rem(k + 1, RING))

            for b in range(batch):
                @pl.loop(0, per_row // GROUP, unroll=7)
                def _(g):
                    sl = pl.ds(pl.multiple_of(b * per_row + g * GROUP, GROUP), GROUP)
                    at = pl.ds(pl.multiple_of(b * (rows * per_row) + row * per_row + g * GROUP, GROUP), GROUP)
                    scale = inverse[pl.ds(pl.multiple_of(g * GROUP, GROUP), GROUP)] * row_scale
                    teach = masked([(planar[before, j, sl] + planar[now, j, sl] + planar[after, j, sl]) * scale for j in range(blocks)])
                    top = jnp.max(fold(teach, jnp.maximum), -1, keepdims=True)
                    teach = [value - top for value in teach]
                    powers = [jnp.exp2(value) for value in teach]
                    norm = jnp.sum(fold(powers, jnp.add), -1, keepdims=True)
                    learn = [value * EXP2_SCALE - shift[at] for value in masked([logits[at, lanes(j)] for j in range(blocks)])]
                    cross = jnp.sum(fold([power * (t - l) for power, t, l in zip(powers, teach, learn)], jnp.add), -1, keepdims=True)
                    total[...] += cross / norm - jnp.log2(norm)
                    weigh = 2.0 / norm
                    for j in range(blocks):
                        slope = jnp.exp2(learn[j] + 1.0) - powers[j] * weigh
                        slopes[at, lanes(j)] = slope.astype(jnp.bfloat16)

    @pl.loop(rows + 2 - RING, rows + 2)
    def _(k):
        edge_copy(k).wait_send()

    dims = 2 + bits
    my_bits = [ta, ha] + [lax.rem(wa // (1 << (bits - 1 - i)), 2) for i in range(bits)]
    chunks = padded // HEAD_CHUNK
    near = 2 + bits - 1

    def order(j):
        first = [1, near] if j % 2 == 0 else [near, 1]
        return [0] + first + [2 + i for i in reversed(range(bits - 1))]

    def partner_of(d):
        if d == 0:
            return {"ta": 1 - ta}
        if d == 1:
            return {"ha": 1 - ha}
        return {"wa": wa + (1 - 2 * my_bits[d]) * (1 << (bits - 1 - (d - 2)))}

    def region(j, s, other):
        seq = order(j)
        index = [slice(None)] * dims
        for d in seq[:s]:
            index[d] = my_bits[d]
        index[seq[s]] = 1 - my_bits[seq[s]] if other else my_bits[seq[s]]
        return (j, *index)

    def red_copy(j, s):
        return pltpu.make_async_remote_copy(
            src_ref=part.at[region(j, s, True)], dst_ref=landed[s].at[j], send_sem=red_send.at[j, s], recv_sem=red_recv.at[j, s],
            device_id=partner_of(order(j)[s]), device_id_type=MESH)

    def head_grad(j):
        half = width // 2
        parts = []
        for h in range(2):
            grad = lax.dot_general(features[:, pl.ds(h * half, half)], slopes[:, pl.ds(j * HEAD_CHUNK, HEAD_CHUNK)],
                                   (((0,), (0,)), ((), ())), preferred_element_type=jnp.float32)
            part[j, h] = grad.astype(part.dtype).reshape(part.shape[2:])
        red_copy(j, 0).start()

    def advance(j, s):
        red_copy(j, s).wait_recv()
        value = part[region(j, s, False)].astype(jnp.float32) + landed[s][j].astype(jnp.float32)
        if s + 1 < dims:
            part[region(j, s, False)] = value.astype(part.dtype)
            red_copy(j, s + 1).start()
        else:
            final[:, pl.ds(j * HEAD_CHUNK, HEAD_CHUNK)] = value

    def out_copy(i):
        return pltpu.make_async_copy(features.at[feat_rows(i)], fgrad.at[feat_rows(i)], out_sem.at[i])

    def feature_grad(i):
        grad = jnp.dot(slopes[feat_rows(i)], head[...], preferred_element_type=jnp.float32)
        features[feat_rows(i)] = grad.astype(features.dtype)
        out_copy(i).start()

    waits = [1.5, 3.2, 2.0] + [1.4] * (dims - 3)
    events = []
    for j in range(chunks):
        ready = 2.3 * (j + 1)
        for s in range(dims):
            ready += waits[s]
            events.append((ready, j, s))
    events.sort()
    clock = 0.0
    for op in [(head_grad, j, 2.3) for j in range(chunks)] + [(feature_grad, i, 1.2) for i in range(fchunks)]:
        op[0](op[1])
        clock += op[2]
        while events and events[0][0] <= clock:
            _, j, s = events.pop(0)
            advance(j, s)
    for _, j, s in events:
        advance(j, s)

    grad = final[...]
    squares = jnp.sum(jnp.sum(grad * grad, axis=1, keepdims=True), axis=0, keepdims=True)
    spent = jnp.sum(total[...], axis=0, keepdims=True) * (sharpness_divisor * sharpness_divisor * math.log(2.0))
    lane = lax.broadcasted_iota(jnp.int32, stat.shape, 1)
    stat[...] = jnp.where(lane == 0, squares, jnp.where(lane == 1, spent, 0.0))

    def stat_copy(k):
        return pltpu.make_async_remote_copy(
            src_ref=stat, dst_ref=stat_in.at[k], send_sem=stat_send.at[k], recv_sem=stat_recv.at[k],
            device_id={"wa": lax.rem(wa + k, n)}, device_id_type=MESH)

    @pl.loop(1, n)
    def _(k):
        stat_copy(k).start()

    stat_in[0] = stat[...]

    @pl.loop(1, n)
    def _(k):
        stat_copy(k).wait_recv()

    stat_out[...] = jnp.sum(stat_in[...], axis=0)
    others = ({"ta": 1 - ta}, {"ha": 1 - ha}, {"ta": 1 - ta, "ha": 1 - ha})
    second = [
        pltpu.make_async_remote_copy(
            src_ref=stat_out, dst_ref=stat_in2.at[k], send_sem=stat_send.at[n + k], recv_sem=stat_recv.at[n + k],
            device_id=device, device_id_type=MESH)
        for k, device in enumerate(others)
    ]
    for copy in second:
        copy.start()
    for copy in second:
        copy.wait_recv()
    lows = [stat_out[...]] + [stat_in2[k] for k in range(3)]
    both = (lows[0] + lows[1]) + (lows[2] + lows[3])
    norm = jnp.sqrt(both[0:1, 0:1])
    loss[...] = both[0:1, 1:2]
    clip = jnp.minimum(1.0, clip_norm / (norm + 1e-06))
    own = own_turned[pl.ds(pl.multiple_of(lax.rem(first_row, LANES), owned), owned)]
    new_weight[...] = own - learn_rate * clip * final[:, pl.ds(0, classes)]

    for copy in second:
        copy.wait_send()

    @pl.loop(1, n)
    def _(k):
        stat_copy(k).wait_send()

    for j in range(chunks):
        for s in range(dims):
            red_copy(j, s).wait_send()

    @pl.loop(0, fchunks)
    def _(i):
        out_copy(i).wait()

    row_copy().wait_send()
    for side in (0, 1):
        @pl.when(sends[side])
        def _():
            corner_copy(side).wait_send()

            @pl.loop(0, col_chunks)
            def _(q):
                col_copy(side, q).wait_send()


def local(features, teacher, head_weight):
    features, teacher = (jnp.transpose(array, (0, 2, 3, 1, 4)) for array in (features, teacher))
    batch, rows, columns, frames, width = features.shape
    classes = teacher.shape[-1]
    tokens = batch * rows * columns * frames
    n = lax.axis_size("wa")
    bits = n.bit_length() - 1
    devices = 4 * n
    owned = width // devices
    padded = -(-classes // HEAD_CHUNK) * HEAD_CHUNK
    chunks = padded // HEAD_CHUNK
    dims = 2 + bits
    outs = batch * columns * frames
    edges = -(-(batch * columns) // 16) * 16
    fchunks = rows // 2
    col_chunks = rows // 2
    f32, bf16 = jnp.float32, jnp.bfloat16
    dma = pltpu.SemaphoreType.DMA
    any_space = pl.BlockSpec(memory_space=pl.ANY)
    vmem = pl.BlockSpec(memory_space=pltpu.VMEM)
    fgrad, loss, new_weight = pl.pallas_call(
        functools.partial(step_kernel, n),
        in_specs=[any_space] * 3,
        out_specs=[any_space, vmem, vmem],
        out_shape=[
            jax.ShapeDtypeStruct((tokens, width), features.dtype),
            jax.ShapeDtypeStruct((1, 1), f32),
            jax.ShapeDtypeStruct((owned, classes), f32),
        ],
        scratch_shapes=[
            pltpu.VMEM((batch, rows + 1, columns + 2, frames, classes), bf16),
            pltpu.VMEM((tokens, width), bf16),
            pltpu.VMEM((tokens, padded), f32),
            pltpu.VMEM((tokens, padded), bf16),
            pltpu.VMEM((padded, width), bf16),
            pltpu.VMEM((RING, padded // LANES, outs + edges, LANES), f32),
            pltpu.VMEM((rows + 2, padded // LANES, edges, LANES), f32),
            pltpu.VMEM((tokens // fchunks, LANES), f32),
            pltpu.VMEM((tokens, LANES), f32),
            pltpu.VMEM((outs + edges, batch * (columns + 2) * frames), bf16),
            pltpu.VMEM((columns * frames, 128), f32),
            pltpu.VMEM((chunks, 2, 2) + (2,) * bits + (owned, HEAD_CHUNK), bf16),
            pltpu.VMEM((owned, padded), f32),
            pltpu.VMEM((classes, LANES), f32),
            pltpu.VMEM((LANES, classes), f32),
            pltpu.VMEM((GROUP, 1), f32),
            pltpu.VMEM((8, 128), f32),
            pltpu.VMEM((n, 8, 128), f32),
            pltpu.VMEM((8, 128), f32),
            pltpu.VMEM((3, 8, 128), f32),
            [pltpu.VMEM((chunks,) + (2,) * (dims - 1 - s) + (owned, HEAD_CHUNK), bf16) for s in range(dims)],
            dma((3,)),
            dma((fchunks,)),
            dma((2, col_chunks)),
            dma((2, col_chunks)),
            dma((3,)),
            dma((3,)),
            dma((RING,)),
            dma((rows + 2,)),
            dma((chunks, dims)),
            dma((chunks, dims)),
            dma((n + 3,)),
            dma((n + 3,)),
            dma((fchunks,)),
        ],
        compiler_params=pltpu.CompilerParams(collective_id=0, has_side_effects=True, vmem_limit_bytes=63 * 1024 * 1024),
    )(teacher, features.reshape(tokens, width), head_weight.T)
    fgrad = jnp.transpose(fgrad.reshape(features.shape), (0, 3, 1, 2, 4))
    return fgrad, loss[0, 0], new_weight


def solution(mesh):
    assert mesh.shape["ta"] == 2 and mesh.shape["ha"] == 2
    placed = (P(None, "ta", "ha", "wa", None), P(None, "ta", "ha", "wa", None), P())
    return jax.shard_map(
        local,
        mesh=mesh,
        in_specs=placed,
        out_specs=(P(None, "ta", "ha", "wa", None), P(), P(AXES, None)),
        check_vma=False,
    )
```

```python
import functools
import math

import jax
import jax.numpy as jnp
from jax import lax
from jax.experimental import pallas as pl
from jax.experimental.pallas import tpu as pltpu
from jax.sharding import PartitionSpec as P

WW = 14
WV = 28
AXES = ("ta", "ha", "wa")
MESH = pl.DeviceIdType.MESH

sharpness_divisor = 2.0
learn_rate = 0.1
clip_norm = 1000.0
EXP2_SCALE = math.log2(math.e) / sharpness_divisor

LAG = 3
RING = LAG + 3
HEAD_ROWS = 4
GROUP = 16
HEAD_CHUNK = 256
LANES = 128
LOW = -1e30


def step_kernel(n, teacher, feats, weight, fgrad, loss, new_weight, cells, features, logits, slopes, head, planar, partner, peak, shift,
                pool, inverse, part, final, own_rows, own_turned, total, stat, stat_in, summed, landed, load_sem, feat_sem, col_send, col_recv, row_send,
                row_recv, edge_send, edge_recv, red_send, red_recv, far_send, far_recv, stat_send, stat_recv, out_sem, hop_sem):
    batch, rows, columns, frames, classes = teacher.shape
    tokens, width = feats.shape
    ta, ha, wa = (lax.axis_index(axis) for axis in AXES)
    per_row = columns * frames
    slots = columns + 2
    sides = slots * frames
    outs = batch * per_row
    edges = planar.shape[2] - outs
    bits = n.bit_length() - 1
    owned = final.shape[0]
    has_left, has_right = wa > 0, wa < n - 1

    barrier = pltpu.get_barrier_semaphore()

    def greet(device):
        pl.semaphore_signal(barrier, inc=1, device_id=device, device_id_type=MESH)

    greet({"ta": 1 - ta})
    greet({"ha": 1 - ha})

    @pl.when(has_left)
    def _():
        greet({"wa": wa - 1})

    @pl.when(has_right)
    def _():
        greet({"wa": wa + 1})

    staged = logits.at[pl.ds(0, classes)]
    head_load = pltpu.make_async_copy(weight, staged, load_sem.at[0])
    head_load.start()
    fchunks = feat_sem.shape[0]
    chunk = tokens // fchunks

    def feat_rows(i):
        return pl.ds(pl.multiple_of(i * chunk, 16), chunk)

    def feat_load(i):
        return pltpu.make_async_copy(feats.at[feat_rows(i)], features.at[feat_rows(i)], feat_sem.at[i])

    @pl.loop(0, fchunks)
    def _(i):
        feat_load(i).start()

    cell_load = pltpu.make_async_copy(teacher, cells.at[:, pl.ds(0, rows), pl.ds(0, columns)], load_sem.at[1])
    cell_load.start()
    mine = (ta * 2 + ha) * n + wa
    first_row = mine * owned
    lane_block = pl.ds(pl.multiple_of(first_row // LANES * LANES, LANES), LANES)
    own_load = pltpu.make_async_copy(weight.at[:, lane_block], own_rows, load_sem.at[2])
    own_load.start()

    pl.semaphore_wait(barrier, 2 + has_left.astype(jnp.int32) + has_right.astype(jnp.int32))

    col_chunks = col_send.shape[1]
    span = rows // col_chunks

    def col_copy(side, q):
        start = jnp.where(ha == 0, q * span, rows - (q + 1) * span)
        at = pl.ds(start, span)
        return pltpu.make_async_remote_copy(
            src_ref=teacher.at[:, at, columns - 1 if side == 0 else 0], dst_ref=cells.at[:, at, columns + side],
            send_sem=col_send.at[side, q], recv_sem=col_recv.at[side, q],
            device_id={"wa": wa + 1 if side == 0 else wa - 1}, device_id_type=MESH)

    facing = jnp.where(ha == 0, rows - 1, 0)

    def row_copy():
        return pltpu.make_async_remote_copy(
            src_ref=teacher.at[:, facing], dst_ref=cells.at[:, rows, pl.ds(0, columns)], send_sem=row_send.at[2], recv_sem=row_recv.at[2],
            device_id={"ha": 1 - ha}, device_id_type=MESH)

    def corner_copy(side):
        return pltpu.make_async_remote_copy(
            src_ref=teacher.at[:, facing, columns - 1 if side == 0 else 0], dst_ref=cells.at[:, rows, columns + side],
            send_sem=row_send.at[side], recv_sem=row_recv.at[side],
            device_id={"ha": 1 - ha, "wa": wa + 1 if side == 0 else wa - 1}, device_id_type=MESH)

    sends = (has_right, has_left)
    gets = (has_left, has_right)

    @pl.loop(0, col_chunks)
    def _(q):
        for side in (0, 1):
            @pl.when(sends[side])
            def _():
                col_copy(side, q).start()

    row_copy().start()

    def tell(r):
        far = 1 << r

        @pl.when(wa >= far)
        def _():
            pl.semaphore_signal(hop_sem.at[r], inc=1, device_id={"wa": wa - far}, device_id_type=MESH)

        @pl.when(wa + far < n)
        def _():
            pl.semaphore_signal(hop_sem.at[r], inc=1, device_id={"wa": wa + far}, device_id_type=MESH)

    def hear(r):
        far = 1 << r
        pl.semaphore_wait(hop_sem.at[r], (wa >= far).astype(jnp.int32) + (wa + far < n).astype(jnp.int32))

    tell(0)

    base = lax.rem(wa * columns + WV - WW // 2, WV)

    def clip_at(col):
        at = col + base
        return jnp.where(at < 0, -1, jnp.where(at >= WV, 1, 0))

    grid_wide = columns * n
    out = lax.broadcasted_iota(jnp.int32, pool.shape, 0)
    src = lax.broadcasted_iota(jnp.int32, pool.shape, 1)
    is_edge = out >= outs
    edge_at = out - outs
    main_batch = (out >= per_row).astype(jnp.int32)
    edge_batch = (edge_at >= columns).astype(jnp.int32)
    out_batch = jnp.where(is_edge, edge_batch, main_batch)
    main_in = out - main_batch * per_row
    out_col = jnp.where(is_edge, edge_at - edge_batch * columns, main_in // frames)
    out_frame = lax.rem(main_in, frames)
    src_batch = (src >= sides).astype(jnp.int32)
    src_in = src - src_batch * sides
    src_slot = src_in // frames
    src_frame = lax.rem(src_in, frames)
    src_col = jnp.where(src_slot == columns, -1, jnp.where(src_slot == columns + 1, columns, src_slot))
    edge_frame = jnp.where(ta == 0, frames - 1, 0)
    src_at = src_col + wa * columns
    away = jnp.where(is_edge, src_frame - edge_frame, src_frame - out_frame)
    reach = jnp.where(is_edge, 0, 1)
    taken = (
        (out_batch == src_batch) & (out_col < columns) & (jnp.abs(out_col - src_col) <= 1) & (jnp.abs(away) <= reach)
        & (src_at >= 0) & (src_at < grid_wide) & (clip_at(out_col) == clip_at(src_col))
    )
    pool[...] = jnp.where(taken, 1.0, 0.0).astype(jnp.bfloat16)
    cell = lax.broadcasted_iota(jnp.int32, inverse.shape, 0)
    col, frame = cell // frames, lax.rem(cell, frames)
    at = col + wa * columns
    left_ok = (at > 0) & (clip_at(col - 1) == clip_at(col))
    right_ok = (at < grid_wide - 1) & (clip_at(col + 1) == clip_at(col))
    frame_at = frame + ta * frames
    frame_edge = (frame_at == 0) | (frame_at == 2 * frames - 1)
    cols = 1.0 + jnp.where(left_ok, 1.0, 0.0) + jnp.where(right_ok, 1.0, 0.0)
    inverse[...] = EXP2_SCALE / (cols * jnp.where(frame_edge, 2.0, 3.0))

    for side in (0, 1):
        @pl.when(jnp.logical_not(gets[side]))
        def _():
            cells[:, :, columns + side] = jnp.zeros((batch, rows + 1, frames, classes), cells.dtype)

    planar[0] = jnp.zeros(planar.shape[1:], jnp.float32)
    summed[...] = jnp.zeros_like(summed)

    padded = head.shape[0]
    blocks = padded // LANES
    head_load.wait()

    @pl.loop(0, blocks)
    def _(i):
        at = pl.ds(pl.multiple_of(i * LANES, LANES), LANES)
        class_at = lax.broadcasted_iota(jnp.int32, (LANES, 1), 0) + i * LANES
        head[at] = jnp.where(class_at < classes, logits[at], 0.0).astype(jnp.bfloat16)

    own_load.wait()
    own_turned[...] = own_rows[...].T

    lane_at = lax.broadcasted_iota(jnp.int32, (GROUP, LANES), 1)
    real = lane_at < classes - (blocks - 1) * LANES

    def lanes(j):
        return pl.ds(j * LANES, LANES)

    def fold(values, op):
        values = list(values)
        while len(values) > 1:
            values = [op(*values[i : i + 2]) if i + 1 < len(values) else values[i] for i in range(0, len(values), 2)]
        return values[0]

    def masked(values):
        return values[:-1] + [jnp.where(real, values[-1], LOW)]

    @pl.loop(0, fchunks)
    def _(i):
        feat_load(i).wait()
        logits[feat_rows(i)] = lax.dot_general(features[feat_rows(i)], head[...], (((1,), (1,)), ((), ())), preferred_element_type=jnp.float32)

        @pl.loop(0, chunk // GROUP, unroll=7)
        def _(g):
            at = pl.ds(pl.multiple_of(i * chunk + g * GROUP, GROUP), GROUP)
            top = jnp.max(fold(masked([logits[at, lanes(j)] for j in range(blocks)]), jnp.maximum), -1, keepdims=True)
            peak[pl.ds(pl.multiple_of(g * GROUP, GROUP), GROUP)] = jnp.broadcast_to(top * EXP2_SCALE, (GROUP, LANES))

        @pl.loop(0, chunk // GROUP, unroll=7)
        def _(g):
            at = pl.ds(pl.multiple_of(i * chunk + g * GROUP, GROUP), GROUP)
            high = peak[pl.ds(pl.multiple_of(g * GROUP, GROUP), GROUP)]
            powers = [jnp.exp2(value * EXP2_SCALE - high) for value in masked([logits[at, lanes(j)] for j in range(blocks)])]
            norm = jnp.sum(fold(powers, jnp.add), -1, keepdims=True)
            shift[at] = high + jnp.log2(norm)

        for r in range(bits):
            @pl.when(i == r)
            def _():
                hear(r)
                if r == 0:
                    for side in (0, 1):
                        @pl.when(sends[side])
                        def _():
                            corner_copy(side).start()
                if r + 1 < bits:
                    tell(r + 1)

    cell_load.wait()
    total[...] = jnp.zeros_like(total)

    def row_of(k):
        return jnp.where(k > rows, rows, jnp.where(ha == 0, k - 1, rows - k))

    def edge_copy(k):
        return pltpu.make_async_remote_copy(
            src_ref=planar.at[lax.rem(k, RING), :, pl.ds(outs, edges)], dst_ref=partner.at[k],
            send_sem=edge_send.at[lax.rem(k, RING)], recv_sem=edge_recv.at[k], device_id={"ta": 1 - ta}, device_id_type=MESH)

    @pl.loop(1, rows + 2 + LAG)
    def _(it):
        @pl.when(it <= rows + 1)
        def _():
            @pl.when((it <= rows) & (lax.rem(it - 1, span) == 0))
            def _():
                for side in (0, 1):
                    @pl.when(gets[side])
                    def _():
                        col_copy(side, (it - 1) // span).wait_recv()

            @pl.when(it == rows + 1)
            def _():
                row_copy().wait_recv()
                for side in (0, 1):
                    @pl.when(gets[side])
                    def _():
                        corner_copy(side).wait_recv()

            @pl.when(it > RING)
            def _():
                edge_copy(it - RING).wait_send()

            here = cells[:, row_of(it)].reshape(batch * sides, classes)
            sums = jnp.dot(pool[...], here, preferred_element_type=jnp.float32)
            for j in range(blocks):
                wide = min(LANES, classes - j * LANES)
                planar[lax.rem(it, RING), j, :, pl.ds(0, wide)] = sums[:, j * LANES : j * LANES + wide]
            edge_copy(it).start()

        @pl.when(it > LAG)
        def _():
            edge_copy(it - LAG).wait_recv()
            slot = lax.rem(it - LAG, RING)
            at = pl.ds(jnp.where(ta == 0, frames - 1, 0), batch * columns, stride=frames)
            for j in range(blocks):
                planar[slot, j, at] += partner[it - LAG, j, pl.ds(0, batch * columns)]

        @pl.when(it > LAG + 1)
        def _():
            k = it - LAG - 1
            row = row_of(k)
            row_at = row + ha * rows
            row_scale = jnp.where((row_at == 0) | (row_at == 2 * rows - 1), 1.0 / 2.0, 1.0 / 3.0)
            before, now, after = (lax.rem(k + RING - 1, RING), lax.rem(k, RING), lax.rem(k + 1, RING))

            for b in range(batch):
                @pl.loop(0, per_row // GROUP, unroll=7)
                def _(g):
                    sl = pl.ds(pl.multiple_of(b * per_row + g * GROUP, GROUP), GROUP)
                    at = pl.ds(pl.multiple_of(b * (rows * per_row) + row * per_row + g * GROUP, GROUP), GROUP)
                    scale = inverse[pl.ds(pl.multiple_of(g * GROUP, GROUP), GROUP)] * row_scale
                    teach = masked([(planar[before, j, sl] + planar[now, j, sl] + planar[after, j, sl]) * scale for j in range(blocks)])
                    top = jnp.max(fold(teach, jnp.maximum), -1, keepdims=True)
                    teach = [value - top for value in teach]
                    powers = [jnp.exp2(value) for value in teach]
                    norm = jnp.sum(fold(powers, jnp.add), -1, keepdims=True)
                    learn = [value * EXP2_SCALE - shift[at] for value in masked([logits[at, lanes(j)] for j in range(blocks)])]
                    cross = jnp.sum(fold([power * (t - l) for power, t, l in zip(powers, teach, learn)], jnp.add), -1, keepdims=True)
                    total[...] += cross / norm - jnp.log2(norm)
                    weigh = 2.0 / norm
                    for j in range(blocks):
                        slope = jnp.exp2(learn[j] + 1.0) - powers[j] * weigh
                        slopes[at, lanes(j)] = slope.astype(jnp.bfloat16)

            @pl.when(lax.rem(k, HEAD_ROWS) == 0)
            def _():
                @pl.loop(0, batch * (width // HEAD_CHUNK))
                def _(i):
                    b = i // (width // HEAD_CHUNK)
                    mine = pl.ds(pl.multiple_of(lax.rem(i, width // HEAD_CHUNK) * HEAD_CHUNK, HEAD_CHUNK), HEAD_CHUNK)
                    first = b * rows + jnp.where(ha == 0, k - HEAD_ROWS, rows - k)
                    at = pl.ds(pl.multiple_of(first * per_row, GROUP), HEAD_ROWS * per_row)
                    summed[mine] += lax.dot_general(features[at, mine], slopes[at], (((0,), (0,)), ((), ())), preferred_element_type=jnp.float32)

    @pl.loop(rows + 2 - RING, rows + 2)
    def _(k):
        edge_copy(k).wait_send()

    far_count = n // 2
    far, low = wa // 2, lax.rem(wa, 2)
    chunks = padded // HEAD_CHUNK
    left_over = rows % HEAD_ROWS
    halvings = 3

    def order(j):
        return (0, 1, 2) if j % 2 == 0 else (0, 2, 1)

    def partner_of(d):
        return ({"ta": 1 - ta}, {"ha": 1 - ha}, {"wa": far * 2 + 1 - low})[d]

    def region(j, s, other):
        seq = order(j)
        index = [slice(None)] * 3
        for d in seq[:s]:
            index[d] = (ta, ha, low)[d]
        own = (ta, ha, low)[seq[s]]
        index[seq[s]] = 1 - own if other else own
        return (j, index[0], index[1], slice(None), index[2])

    def landing(j, s):
        return landed[s].at[j] if s != 1 else landed[1 if j % 2 == 0 else 4].at[j // 2]

    def red_copy(j, s):
        return pltpu.make_async_remote_copy(
            src_ref=part.at[region(j, s, True)], dst_ref=landing(j, s), send_sem=red_send.at[j, s], recv_sem=red_recv.at[j, s],
            device_id=partner_of(order(j)[s]), device_id_type=MESH)

    def far_copy(j, k):
        to = lax.rem(far + k, far_count)
        return pltpu.make_async_remote_copy(
            src_ref=part.at[j, ta, ha, to, low], dst_ref=landed[halvings].at[j, k], send_sem=far_send.at[j, k], recv_sem=far_recv.at[j, k],
            device_id={"wa": to * 2 + low}, device_id_type=MESH)

    def head_grad(j):
        half = width // 2
        columns_at = pl.ds(j * HEAD_CHUNK, HEAD_CHUNK)
        for h in range(2):
            grad = summed[pl.ds(h * half, half), columns_at]
            if left_over:
                for b in range(batch):
                    at = pl.ds(pl.multiple_of((b * rows + jnp.where(ha == 0, rows - left_over, 0)) * per_row, GROUP), left_over * per_row)
                    grad += lax.dot_general(features[at, pl.ds(h * half, half)], slopes[at, columns_at],
                                            (((0,), (0,)), ((), ())), preferred_element_type=jnp.float32)
            part[j, h] = grad.astype(part.dtype).reshape(part.shape[2:])
        red_copy(j, 0).start()

    def advance(j, s):
        if s < halvings:
            red_copy(j, s).wait_recv()
            part[region(j, s, False)] = (part[region(j, s, False)].astype(jnp.float32) + landing(j, s)[...].astype(jnp.float32)).astype(part.dtype)
            if s + 1 < halvings:
                red_copy(j, s + 1).start()
            else:
                @pl.loop(1, far_count)
                def _(k):
                    far_copy(j, k).start()
        else:
            columns_at = pl.ds(j * HEAD_CHUNK, HEAD_CHUNK)
            final[:, columns_at] = part[j, ta, ha, far, low].astype(jnp.float32)

            @pl.loop(1, far_count)
            def _(k):
                far_copy(j, k).wait_recv()
                final[:, columns_at] += landed[halvings][j, k].astype(jnp.float32)

    def out_copy(i):
        return pltpu.make_async_copy(features.at[feat_rows(i)], fgrad.at[feat_rows(i)], out_sem.at[i])

    def feature_grad(i):
        grad = jnp.dot(slopes[feat_rows(i)], head[...], preferred_element_type=jnp.float32)
        features[feat_rows(i)] = grad.astype(features.dtype)
        out_copy(i).start()

    begin = [(3.0, 1.0), (8.0, 1.5), (12.0, 1.2), (16.0, 0.8)]
    events = sorted((base + more * j, s, j) for s, (base, more) in enumerate(begin) for j in range(chunks))
    clock = 0.0
    for op in [(head_grad, j, 0.5) for j in range(chunks)] + [(feature_grad, i, 1.2) for i in range(fchunks)]:
        op[0](op[1])
        clock += op[2]
        while events and events[0][0] <= clock:
            _, s, j = events.pop(0)
            advance(j, s)
    for _, s, j in events:
        advance(j, s)

    grad = final[...]
    squares = jnp.sum(jnp.sum(grad * grad, axis=1, keepdims=True), axis=0, keepdims=True)
    spent = jnp.sum(total[...], axis=0, keepdims=True) * (sharpness_divisor * sharpness_divisor * math.log(2.0))
    lane = lax.broadcasted_iota(jnp.int32, stat.shape, 1)
    stat[...] = jnp.where(lane == 0, squares, jnp.where(lane == 1, spent, 0.0))

    def stat_copy(k):
        to = lax.rem(mine + k, 4 * n)
        return pltpu.make_async_remote_copy(
            src_ref=stat, dst_ref=stat_in.at[mine], send_sem=stat_send.at[k], recv_sem=stat_recv.at[k],
            device_id={"ta": to // (2 * n), "ha": lax.rem(to // n, 2), "wa": lax.rem(to, n)}, device_id_type=MESH)

    @pl.loop(1, 4 * n)
    def _(k):
        stat_copy(k).start()

    stat_in[mine] = stat[...]

    @pl.loop(1, 4 * n)
    def _(k):
        stat_copy(k).wait_recv()

    both = jnp.sum(stat_in[...], axis=0)
    norm = jnp.sqrt(both[0:1, 0:1])
    loss[...] = both[0:1, 1:2]
    clip = jnp.minimum(1.0, clip_norm / (norm + 1e-06))
    own = own_turned[pl.ds(pl.multiple_of(lax.rem(first_row, LANES), owned), owned)]
    new_weight[...] = own - learn_rate * clip * final[:, pl.ds(0, classes)]

    @pl.loop(1, 4 * n)
    def _(k):
        stat_copy(k).wait_send()

    for j in range(chunks):
        for s in range(halvings):
            red_copy(j, s).wait_send()

        @pl.loop(1, far_count)
        def _(k):
            far_copy(j, k).wait_send()

    @pl.loop(0, fchunks)
    def _(i):
        out_copy(i).wait()

    row_copy().wait_send()
    for side in (0, 1):
        @pl.when(sends[side])
        def _():
            corner_copy(side).wait_send()

            @pl.loop(0, col_chunks)
            def _(q):
                col_copy(side, q).wait_send()


def local(features, teacher, head_weight):
    features, teacher = (jnp.transpose(array, (0, 2, 3, 1, 4)) for array in (features, teacher))
    batch, rows, columns, frames, width = features.shape
    classes = teacher.shape[-1]
    tokens = batch * rows * columns * frames
    n = lax.axis_size("wa")
    bits = n.bit_length() - 1
    devices = 4 * n
    owned = width // devices
    padded = -(-classes // HEAD_CHUNK) * HEAD_CHUNK
    chunks = padded // HEAD_CHUNK
    outs = batch * columns * frames
    edges = -(-(batch * columns) // 16) * 16
    fchunks = rows // 2
    col_chunks = rows // 2
    f32, bf16 = jnp.float32, jnp.bfloat16
    dma = pltpu.SemaphoreType.DMA
    any_space = pl.BlockSpec(memory_space=pl.ANY)
    vmem = pl.BlockSpec(memory_space=pltpu.VMEM)
    fgrad, loss, new_weight = pl.pallas_call(
        functools.partial(step_kernel, n),
        in_specs=[any_space] * 3,
        out_specs=[any_space, vmem, vmem],
        out_shape=[
            jax.ShapeDtypeStruct((tokens, width), features.dtype),
            jax.ShapeDtypeStruct((1, 1), f32),
            jax.ShapeDtypeStruct((owned, classes), f32),
        ],
        scratch_shapes=[
            pltpu.VMEM((batch, rows + 1, columns + 2, frames, classes), bf16),
            pltpu.VMEM((tokens, width), bf16),
            pltpu.VMEM((tokens, padded), f32),
            pltpu.VMEM((tokens, padded), bf16),
            pltpu.VMEM((padded, width), bf16),
            pltpu.VMEM((RING, padded // LANES, outs + edges, LANES), f32),
            pltpu.VMEM((rows + 2, padded // LANES, edges, LANES), f32),
            pltpu.VMEM((tokens // fchunks, LANES), f32),
            pltpu.VMEM((tokens, LANES), f32),
            pltpu.VMEM((outs + edges, batch * (columns + 2) * frames), bf16),
            pltpu.VMEM((columns * frames, 128), f32),
            pltpu.VMEM((chunks, 2, 2, n // 2, 2, owned, HEAD_CHUNK), bf16),
            pltpu.VMEM((owned, padded), f32),
            pltpu.VMEM((classes, LANES), f32),
            pltpu.VMEM((LANES, classes), f32),
            pltpu.VMEM((GROUP, 1), f32),
            pltpu.VMEM((8, 128), f32),
            pltpu.VMEM((devices, 8, 128), f32),
            pltpu.VMEM((width, padded), f32),
            [pltpu.VMEM(shape + (owned, HEAD_CHUNK), bf16) for shape in (
                (chunks, 2, n // 2, 2), ((chunks + 1) // 2, n // 2, 2), (chunks, n // 2), (chunks, n // 2), ((chunks + 1) // 2, 2, n // 2))],
            dma((3,)),
            dma((fchunks,)),
            dma((2, col_chunks)),
            dma((2, col_chunks)),
            dma((3,)),
            dma((3,)),
            dma((RING,)),
            dma((rows + 2,)),
            dma((chunks, 3)),
            dma((chunks, 3)),
            dma((chunks, n // 2)),
            dma((chunks, n // 2)),
            dma((devices,)),
            dma((devices,)),
            dma((fchunks,)),
            pltpu.SemaphoreType.REGULAR((bits,)),
        ],
        compiler_params=pltpu.CompilerParams(collective_id=0, has_side_effects=True, vmem_limit_bytes=63 * 1024 * 1024),
    )(teacher, features.reshape(tokens, width), head_weight.T)
    fgrad = jnp.transpose(fgrad.reshape(features.shape), (0, 3, 1, 2, 4))
    return fgrad, loss[0, 0], new_weight


def solution(mesh):
    assert mesh.shape["ta"] == 2 and mesh.shape["ha"] == 2
    placed = (P(None, "ta", "ha", "wa", None), P(None, "ta", "ha", "wa", None), P())
    return jax.shard_map(
        local,
        mesh=mesh,
        in_specs=placed,
        out_specs=(P(None, "ta", "ha", "wa", None), P(), P(AXES, None)),
        check_vma=False,
    )
```

```python
import functools
import math

import jax
import jax.numpy as jnp
from jax import lax
from jax.experimental import pallas as pl
from jax.experimental.pallas import tpu as pltpu
from jax.sharding import PartitionSpec as P

WW = 14
WV = 28
AXES = ("ta", "ha", "wa")
MESH = pl.DeviceIdType.MESH

sharpness_divisor = 2.0
learn_rate = 0.1
clip_norm = 1000.0
EXP2_SCALE = math.log2(math.e) / sharpness_divisor

LAG = 3
RING = LAG + 3
GROUP = 16
HEAD_CHUNK = 256
LANES = 128
LOW = -1e30
PACE = (0, 0, 1, 3, 4, 6, 6)


def step_kernel(n, teacher, feats, weight, fgrad, loss, new_weight, cells, features, logits, slopes, head, planar, partner, peak, shift,
                pool, inverse, part, final, own_rows, own_turned, total, stat, stat_in, landed, load_sem, feat_sem, col_send, col_recv, row_send,
                row_recv, edge_send, edge_recv, red_send, red_recv, far_send, far_recv, stat_send, stat_recv, out_sem, hop_sem):
    batch, rows, columns, frames, classes = teacher.shape
    tokens, width = feats.shape
    ta, ha, wa = (lax.axis_index(axis) for axis in AXES)
    per_row = columns * frames
    slots = columns + 2
    sides = slots * frames
    outs = batch * per_row
    edges = planar.shape[2] - outs
    bits = n.bit_length() - 1
    owned = final.shape[0]
    has_left, has_right = wa > 0, wa < n - 1

    barrier = pltpu.get_barrier_semaphore()

    def greet(device):
        pl.semaphore_signal(barrier, inc=1, device_id=device, device_id_type=MESH)

    greet({"ta": 1 - ta})
    greet({"ha": 1 - ha})

    @pl.when(has_left)
    def _():
        greet({"wa": wa - 1})

    @pl.when(has_right)
    def _():
        greet({"wa": wa + 1})

    staged = logits.at[pl.ds(0, classes)]
    head_load = pltpu.make_async_copy(weight, staged, load_sem.at[0])
    head_load.start()
    fchunks = feat_sem.shape[0]
    chunk = tokens // fchunks

    def feat_rows(i):
        return pl.ds(pl.multiple_of(i * chunk, 16), chunk)

    def feat_load(i):
        return pltpu.make_async_copy(feats.at[feat_rows(i)], features.at[feat_rows(i)], feat_sem.at[i])

    @pl.loop(0, fchunks)
    def _(i):
        feat_load(i).start()

    cell_load = pltpu.make_async_copy(teacher, cells.at[:, pl.ds(0, rows), pl.ds(0, columns)], load_sem.at[1])
    cell_load.start()
    mine = (ta * 2 + ha) * n + wa
    first_row = mine * owned
    lane_block = pl.ds(pl.multiple_of(first_row // LANES * LANES, LANES), LANES)
    own_load = pltpu.make_async_copy(weight.at[:, lane_block], own_rows, load_sem.at[2])
    own_load.start()

    sends = (has_right, has_left)
    gets = (has_left, has_right)

    base = lax.rem(wa * columns + WV - WW // 2, WV)

    def clip_at(col):
        at = col + base
        return jnp.where(at < 0, -1, jnp.where(at >= WV, 1, 0))

    grid_wide = columns * n
    out = lax.broadcasted_iota(jnp.int32, pool.shape, 0)
    src = lax.broadcasted_iota(jnp.int32, pool.shape, 1)
    is_edge = out >= outs
    edge_at = out - outs
    main_batch = (out >= per_row).astype(jnp.int32)
    edge_batch = (edge_at >= columns).astype(jnp.int32)
    out_batch = jnp.where(is_edge, edge_batch, main_batch)
    main_in = out - main_batch * per_row
    out_col = jnp.where(is_edge, edge_at - edge_batch * columns, main_in // frames)
    out_frame = lax.rem(main_in, frames)
    src_batch = (src >= sides).astype(jnp.int32)
    src_in = src - src_batch * sides
    src_slot = src_in // frames
    src_frame = lax.rem(src_in, frames)
    src_col = jnp.where(src_slot == columns, -1, jnp.where(src_slot == columns + 1, columns, src_slot))
    edge_frame = jnp.where(ta == 0, frames - 1, 0)
    src_at = src_col + wa * columns
    away = jnp.where(is_edge, src_frame - edge_frame, src_frame - out_frame)
    reach = jnp.where(is_edge, 0, 1)
    taken = (
        (out_batch == src_batch) & (out_col < columns) & (jnp.abs(out_col - src_col) <= 1) & (jnp.abs(away) <= reach)
        & (src_at >= 0) & (src_at < grid_wide) & (clip_at(out_col) == clip_at(src_col))
    )
    pool[...] = jnp.where(taken, 1.0, 0.0).astype(jnp.bfloat16)
    cell = lax.broadcasted_iota(jnp.int32, inverse.shape, 0)
    col, frame = cell // frames, lax.rem(cell, frames)
    at = col + wa * columns
    left_ok = (at > 0) & (clip_at(col - 1) == clip_at(col))
    right_ok = (at < grid_wide - 1) & (clip_at(col + 1) == clip_at(col))
    frame_at = frame + ta * frames
    frame_edge = (frame_at == 0) | (frame_at == 2 * frames - 1)
    cols = 1.0 + jnp.where(left_ok, 1.0, 0.0) + jnp.where(right_ok, 1.0, 0.0)
    inverse[...] = EXP2_SCALE / (cols * jnp.where(frame_edge, 2.0, 3.0))

    for side in (0, 1):
        @pl.when(jnp.logical_not(gets[side]))
        def _():
            cells[:, :, columns + side] = jnp.zeros((batch, rows + 1, frames, classes), cells.dtype)

    planar[0] = jnp.zeros(planar.shape[1:], jnp.float32)

    padded = head.shape[0]
    blocks = padded // LANES
    head_load.wait()

    @pl.loop(0, blocks)
    def _(i):
        at = pl.ds(pl.multiple_of(i * LANES, LANES), LANES)
        class_at = lax.broadcasted_iota(jnp.int32, (LANES, 1), 0) + i * LANES
        head[at] = jnp.where(class_at < classes, logits[at], 0.0).astype(jnp.bfloat16)

    own_load.wait()
    own_turned[...] = own_rows[...].T

    pl.semaphore_wait(barrier, 2 + has_left.astype(jnp.int32) + has_right.astype(jnp.int32))

    col_chunks = col_send.shape[1]
    span = rows // col_chunks

    def col_copy(side, q):
        start = jnp.where(ha == 0, q * span, rows - (q + 1) * span)
        at = pl.ds(start, span)
        return pltpu.make_async_remote_copy(
            src_ref=teacher.at[:, at, columns - 1 if side == 0 else 0], dst_ref=cells.at[:, at, columns + side],
            send_sem=col_send.at[side, q], recv_sem=col_recv.at[side, q],
            device_id={"wa": wa + 1 if side == 0 else wa - 1}, device_id_type=MESH)

    facing = jnp.where(ha == 0, rows - 1, 0)

    def row_copy():
        return pltpu.make_async_remote_copy(
            src_ref=teacher.at[:, facing], dst_ref=cells.at[:, rows, pl.ds(0, columns)], send_sem=row_send.at[2], recv_sem=row_recv.at[2],
            device_id={"ha": 1 - ha}, device_id_type=MESH)

    def corner_copy(side):
        return pltpu.make_async_remote_copy(
            src_ref=teacher.at[:, facing, columns - 1 if side == 0 else 0], dst_ref=cells.at[:, rows, columns + side],
            send_sem=row_send.at[side], recv_sem=row_recv.at[side],
            device_id={"ha": 1 - ha, "wa": wa + 1 if side == 0 else wa - 1}, device_id_type=MESH)


    def start_columns(q):
        for side in (0, 1):
            @pl.when(sends[side])
            def _():
                col_copy(side, q).start()

    start_columns(0)
    start_columns(1)
    row_copy().start()

    def tell(r):
        far = 1 << r

        @pl.when(wa >= far)
        def _():
            pl.semaphore_signal(hop_sem.at[r], inc=1, device_id={"wa": wa - far}, device_id_type=MESH)

        @pl.when(wa + far < n)
        def _():
            pl.semaphore_signal(hop_sem.at[r], inc=1, device_id={"wa": wa + far}, device_id_type=MESH)

    def hear(r):
        far = 1 << r
        pl.semaphore_wait(hop_sem.at[r], (wa >= far).astype(jnp.int32) + (wa + far < n).astype(jnp.int32))

    tell(0)

    lane_at = lax.broadcasted_iota(jnp.int32, (GROUP, LANES), 1)
    real = lane_at < classes - (blocks - 1) * LANES

    def lanes(j):
        return pl.ds(j * LANES, LANES)

    def fold(values, op):
        values = list(values)
        while len(values) > 1:
            values = [op(*values[i : i + 2]) if i + 1 < len(values) else values[i] for i in range(0, len(values), 2)]
        return values[0]

    def masked(values):
        return values[:-1] + [jnp.where(real, values[-1], LOW)]

    @pl.loop(0, fchunks)
    def _(i):
        feat_load(i).wait()
        for q in range(2, col_chunks):
            @pl.when(i == min(PACE[min(q, len(PACE) - 1)], fchunks - 1))
            def _():
                start_columns(q)

        logits[feat_rows(i)] = lax.dot_general(features[feat_rows(i)], head[...], (((1,), (1,)), ((), ())), preferred_element_type=jnp.float32)

        @pl.loop(0, chunk // GROUP, unroll=7)
        def _(g):
            at = pl.ds(pl.multiple_of(i * chunk + g * GROUP, GROUP), GROUP)
            top = jnp.max(fold(masked([logits[at, lanes(j)] for j in range(blocks)]), jnp.maximum), -1, keepdims=True)
            peak[pl.ds(pl.multiple_of(g * GROUP, GROUP), GROUP)] = jnp.broadcast_to(top * EXP2_SCALE, (GROUP, LANES))

        @pl.loop(0, chunk // GROUP, unroll=7)
        def _(g):
            at = pl.ds(pl.multiple_of(i * chunk + g * GROUP, GROUP), GROUP)
            high = peak[pl.ds(pl.multiple_of(g * GROUP, GROUP), GROUP)]
            powers = [jnp.exp2(value * EXP2_SCALE - high) for value in masked([logits[at, lanes(j)] for j in range(blocks)])]
            norm = jnp.sum(fold(powers, jnp.add), -1, keepdims=True)
            shift[at] = high + jnp.log2(norm)

        for r in range(bits):
            @pl.when(i == r)
            def _():
                hear(r)
                if r == 0:
                    for side in (0, 1):
                        @pl.when(sends[side])
                        def _():
                            corner_copy(side).start()
                if r + 1 < bits:
                    tell(r + 1)

    cell_load.wait()
    total[...] = jnp.zeros_like(total)

    def row_of(k):
        return jnp.where(k > rows, rows, jnp.where(ha == 0, k - 1, rows - k))

    def edge_copy(k):
        return pltpu.make_async_remote_copy(
            src_ref=planar.at[lax.rem(k, RING), :, pl.ds(outs, edges)], dst_ref=partner.at[k],
            send_sem=edge_send.at[lax.rem(k, RING)], recv_sem=edge_recv.at[k], device_id={"ta": 1 - ta}, device_id_type=MESH)

    @pl.loop(1, rows + 2 + LAG)
    def _(it):
        @pl.when(it <= rows + 1)
        def _():
            @pl.when((it <= rows) & (lax.rem(it - 1, span) == 0))
            def _():
                for side in (0, 1):
                    @pl.when(gets[side])
                    def _():
                        col_copy(side, (it - 1) // span).wait_recv()

            @pl.when(it == rows + 1)
            def _():
                row_copy().wait_recv()
                for side in (0, 1):
                    @pl.when(gets[side])
                    def _():
                        corner_copy(side).wait_recv()

            @pl.when(it > RING)
            def _():
                edge_copy(it - RING).wait_send()

            here = cells[:, row_of(it)].reshape(batch * sides, classes)
            sums = jnp.dot(pool[...], here, preferred_element_type=jnp.float32)
            for j in range(blocks):
                wide = min(LANES, classes - j * LANES)
                planar[lax.rem(it, RING), j, :, pl.ds(0, wide)] = sums[:, j * LANES : j * LANES + wide]
            edge_copy(it).start()

        @pl.when(it > LAG)
        def _():
            edge_copy(it - LAG).wait_recv()
            slot = lax.rem(it - LAG, RING)
            at = pl.ds(jnp.where(ta == 0, frames - 1, 0), batch * columns, stride=frames)
            for j in range(blocks):
                planar[slot, j, at] += partner[it - LAG, j, pl.ds(0, batch * columns)]

        @pl.when(it > LAG + 1)
        def _():
            k = it - LAG - 1
            row = row_of(k)
            row_at = row + ha * rows
            row_scale = jnp.where((row_at == 0) | (row_at == 2 * rows - 1), 1.0 / 2.0, 1.0 / 3.0)
            before, now, after = (lax.rem(k + RING - 1, RING), lax.rem(k, RING), lax.rem(k + 1, RING))

            for b in range(batch):
                @pl.loop(0, per_row // GROUP, unroll=7)
                def _(g):
                    sl = pl.ds(pl.multiple_of(b * per_row + g * GROUP, GROUP), GROUP)
                    at = pl.ds(pl.multiple_of(b * (rows * per_row) + row * per_row + g * GROUP, GROUP), GROUP)
                    scale = inverse[pl.ds(pl.multiple_of(g * GROUP, GROUP), GROUP)] * row_scale
                    teach = masked([(planar[before, j, sl] + planar[now, j, sl] + planar[after, j, sl]) * scale for j in range(blocks)])
                    top = jnp.max(fold(teach, jnp.maximum), -1, keepdims=True)
                    teach = [value - top for value in teach]
                    powers = [jnp.exp2(value) for value in teach]
                    norm = jnp.sum(fold(powers, jnp.add), -1, keepdims=True)
                    learn = [value * EXP2_SCALE - shift[at] for value in masked([logits[at, lanes(j)] for j in range(blocks)])]
                    cross = jnp.sum(fold([power * (t - l) for power, t, l in zip(powers, teach, learn)], jnp.add), -1, keepdims=True)
                    total[...] += cross / norm - jnp.log2(norm)
                    weigh = 2.0 / norm
                    for j in range(blocks):
                        slope = jnp.exp2(learn[j] + 1.0) - powers[j] * weigh
                        slopes[at, lanes(j)] = slope.astype(jnp.bfloat16)

    @pl.loop(rows + 2 - RING, rows + 2)
    def _(k):
        edge_copy(k).wait_send()

    far_count = n // 2
    far, low = wa // 2, lax.rem(wa, 2)
    chunks = padded // HEAD_CHUNK
    halvings = 3

    def order(j):
        return (0, 1, 2) if j % 2 == 0 else (0, 2, 1)

    def partner_of(d):
        return ({"ta": 1 - ta}, {"ha": 1 - ha}, {"wa": far * 2 + 1 - low})[d]

    def region(j, s, other):
        seq = order(j)
        index = [slice(None)] * 3
        for d in seq[:s]:
            index[d] = (ta, ha, low)[d]
        own = (ta, ha, low)[seq[s]]
        index[seq[s]] = 1 - own if other else own
        return (j, index[0], index[1], slice(None), index[2])

    def landing(j, s):
        return landed[s].at[j] if s != 1 else landed[1 if j % 2 == 0 else 4].at[j // 2]

    def red_copy(j, s):
        return pltpu.make_async_remote_copy(
            src_ref=part.at[region(j, s, True)], dst_ref=landing(j, s), send_sem=red_send.at[j, s], recv_sem=red_recv.at[j, s],
            device_id=partner_of(order(j)[s]), device_id_type=MESH)

    def far_copy(j, k):
        to = lax.rem(far + k, far_count)
        return pltpu.make_async_remote_copy(
            src_ref=part.at[j, ta, ha, to, low], dst_ref=landed[halvings].at[j, k], send_sem=far_send.at[j, k], recv_sem=far_recv.at[j, k],
            device_id={"wa": to * 2 + low}, device_id_type=MESH)

    def head_grad(j, first):
        half = width // 2
        h = 1 - ta if first else ta
        grad = lax.dot_general(slopes[:, pl.ds(j * HEAD_CHUNK, HEAD_CHUNK)], features[:, pl.ds(pl.multiple_of(h * half, half), half)],
                               (((0,), (0,)), ((), ())), preferred_element_type=jnp.float32)
        part[j, h] = grad.astype(part.dtype).T.reshape(part.shape[2:])
        if first:
            red_copy(j, 0).start()

    def advance(j, s):
        if s < halvings:
            red_copy(j, s).wait_recv()
            part[region(j, s, False)] = (part[region(j, s, False)].astype(jnp.float32) + landing(j, s)[...].astype(jnp.float32)).astype(part.dtype)
            if s + 1 < halvings:
                red_copy(j, s + 1).start()
            else:
                @pl.loop(1, far_count)
                def _(k):
                    far_copy(j, k).start()
        else:
            columns_at = pl.ds(j * HEAD_CHUNK, HEAD_CHUNK)
            final[:, columns_at] = part[j, ta, ha, far, low].astype(jnp.float32)

            @pl.loop(1, far_count)
            def _(k):
                far_copy(j, k).wait_recv()
                final[:, columns_at] += landed[halvings][j, k].astype(jnp.float32)

    def out_copy(i):
        return pltpu.make_async_copy(features.at[feat_rows(i)], fgrad.at[feat_rows(i)], out_sem.at[i])

    def feature_grad(i):
        grad = jnp.dot(slopes[feat_rows(i)], head[...], preferred_element_type=jnp.float32)
        features[feat_rows(i)] = grad.astype(features.dtype)
        out_copy(i).start()

    begin = [(4.0, 2.5), (7.5, 2.5), (10.0, 2.5), (13.0, 2.3)]
    events = sorted((base + more * j, s, j) for s, (base, more) in enumerate(begin) for j in range(chunks))
    clock = 0.0
    work = [(functools.partial(head_grad, j, first), 1.25) for j in range(chunks) for first in (True, False)]
    work += [(functools.partial(feature_grad, i), 1.2) for i in range(fchunks)]
    for op, cost in work:
        op()
        clock += cost
        while events and events[0][0] <= clock:
            _, s, j = events.pop(0)
            advance(j, s)
    for _, s, j in events:
        advance(j, s)

    grad = final[...]
    squares = jnp.sum(jnp.sum(grad * grad, axis=1, keepdims=True), axis=0, keepdims=True)
    spent = jnp.sum(total[...], axis=0, keepdims=True) * (sharpness_divisor * sharpness_divisor * math.log(2.0))
    lane = lax.broadcasted_iota(jnp.int32, stat.shape, 1)
    stat[...] = jnp.where(lane == 0, squares, jnp.where(lane == 1, spent, 0.0))

    def stat_copy(k):
        to = lax.rem(mine + k, 4 * n)
        return pltpu.make_async_remote_copy(
            src_ref=stat, dst_ref=stat_in.at[mine], send_sem=stat_send.at[k], recv_sem=stat_recv.at[k],
            device_id={"ta": to // (2 * n), "ha": lax.rem(to // n, 2), "wa": lax.rem(to, n)}, device_id_type=MESH)

    @pl.loop(1, 4 * n)
    def _(k):
        stat_copy(k).start()

    stat_in[mine] = stat[...]

    @pl.loop(1, 4 * n)
    def _(k):
        stat_copy(k).wait_recv()

    both = jnp.sum(stat_in[...], axis=0)
    norm = jnp.sqrt(both[0:1, 0:1])
    loss[...] = both[0:1, 1:2]
    clip = jnp.minimum(1.0, clip_norm / (norm + 1e-06))
    own = own_turned[pl.ds(pl.multiple_of(lax.rem(first_row, LANES), owned), owned)]
    new_weight[...] = own - learn_rate * clip * final[:, pl.ds(0, classes)]

    @pl.loop(1, 4 * n)
    def _(k):
        stat_copy(k).wait_send()

    for j in range(chunks):
        for s in range(halvings):
            red_copy(j, s).wait_send()

        @pl.loop(1, far_count)
        def _(k):
            far_copy(j, k).wait_send()

    @pl.loop(0, fchunks)
    def _(i):
        out_copy(i).wait()

    row_copy().wait_send()
    for side in (0, 1):
        @pl.when(sends[side])
        def _():
            corner_copy(side).wait_send()

            @pl.loop(0, col_chunks)
            def _(q):
                col_copy(side, q).wait_send()


def local(features, teacher, head_weight):
    features, teacher = (jnp.transpose(array, (0, 2, 3, 1, 4)) for array in (features, teacher))
    batch, rows, columns, frames, width = features.shape
    classes = teacher.shape[-1]
    tokens = batch * rows * columns * frames
    n = lax.axis_size("wa")
    bits = n.bit_length() - 1
    devices = 4 * n
    owned = width // devices
    padded = -(-classes // HEAD_CHUNK) * HEAD_CHUNK
    chunks = padded // HEAD_CHUNK
    outs = batch * columns * frames
    edges = -(-(batch * columns) // 16) * 16
    fchunks = rows // 2
    col_chunks = rows // 2
    f32, bf16 = jnp.float32, jnp.bfloat16
    dma = pltpu.SemaphoreType.DMA
    any_space = pl.BlockSpec(memory_space=pl.ANY)
    vmem = pl.BlockSpec(memory_space=pltpu.VMEM)
    fgrad, loss, new_weight = pl.pallas_call(
        functools.partial(step_kernel, n),
        in_specs=[any_space] * 3,
        out_specs=[any_space, vmem, vmem],
        out_shape=[
            jax.ShapeDtypeStruct((tokens, width), features.dtype),
            jax.ShapeDtypeStruct((1, 1), f32),
            jax.ShapeDtypeStruct((owned, classes), f32),
        ],
        scratch_shapes=[
            pltpu.VMEM((batch, rows + 1, columns + 2, frames, classes), bf16),
            pltpu.VMEM((tokens, width), bf16),
            pltpu.VMEM((tokens, padded), f32),
            pltpu.VMEM((tokens, padded), bf16),
            pltpu.VMEM((padded, width), bf16),
            pltpu.VMEM((RING, padded // LANES, outs + edges, LANES), f32),
            pltpu.VMEM((rows + 2, padded // LANES, edges, LANES), f32),
            pltpu.VMEM((tokens // fchunks, LANES), f32),
            pltpu.VMEM((tokens, LANES), f32),
            pltpu.VMEM((outs + edges, batch * (columns + 2) * frames), bf16),
            pltpu.VMEM((columns * frames, 128), f32),
            pltpu.VMEM((chunks, 2, 2, n // 2, 2, owned, HEAD_CHUNK), bf16),
            pltpu.VMEM((owned, padded), f32),
            pltpu.VMEM((classes, LANES), f32),
            pltpu.VMEM((LANES, classes), f32),
            pltpu.VMEM((GROUP, 1), f32),
            pltpu.VMEM((8, 128), f32),
            pltpu.VMEM((devices, 8, 128), f32),
            [pltpu.VMEM(shape + (owned, HEAD_CHUNK), bf16) for shape in (
                (chunks, 2, n // 2, 2), ((chunks + 1) // 2, n // 2, 2), (chunks, n // 2), (chunks, n // 2), ((chunks + 1) // 2, 2, n // 2))],
            dma((3,)),
            dma((fchunks,)),
            dma((2, col_chunks)),
            dma((2, col_chunks)),
            dma((3,)),
            dma((3,)),
            dma((RING,)),
            dma((rows + 2,)),
            dma((chunks, 3)),
            dma((chunks, 3)),
            dma((chunks, n // 2)),
            dma((chunks, n // 2)),
            dma((devices,)),
            dma((devices,)),
            dma((fchunks,)),
            pltpu.SemaphoreType.REGULAR((bits,)),
        ],
        compiler_params=pltpu.CompilerParams(collective_id=0, has_side_effects=True, vmem_limit_bytes=63 * 1024 * 1024),
    )(teacher, features.reshape(tokens, width), head_weight.T)
    fgrad = jnp.transpose(fgrad.reshape(features.shape), (0, 3, 1, 2, 4))
    return fgrad, loss[0, 0], new_weight


def solution(mesh):
    assert mesh.shape["ta"] == 2 and mesh.shape["ha"] == 2
    placed = (P(None, "ta", "ha", "wa", None), P(None, "ta", "ha", "wa", None), P())
    return jax.shard_map(
        local,
        mesh=mesh,
        in_specs=placed,
        out_specs=(P(None, "ta", "ha", "wa", None), P(), P(AXES, None)),
        check_vma=False,
    )
```

```python
import functools
import math

import jax
import jax.numpy as jnp
from jax import lax
from jax.experimental import pallas as pl
from jax.experimental.pallas import tpu as pltpu
from jax.sharding import PartitionSpec as P

WW = 14
WV = 28
AXES = ("ta", "ha", "wa")
MESH = pl.DeviceIdType.MESH

sharpness_divisor = 2.0
learn_rate = 0.1
clip_norm = 1000.0
EXP2_SCALE = math.log2(math.e) / sharpness_divisor

LAG = 3
RING = LAG + 3
GROUP = 16
HEAD_CHUNK = 256
LANES = 128
LOW = -1e30
PACE = (0, 0, 1, 3, 4, 6, 6)


def step_kernel(n, teacher, feats, weight, fgrad, loss, new_weight, cells, features, logits, slopes, head, planar, partner, peak, shift,
                pool, inverse, part, final, own_rows, own_turned, total, stat, stat_in, landed, load_sem, feat_sem, col_send, col_recv, row_send,
                row_recv, edge_send, edge_recv, red_send, red_recv, far_send, far_recv, stat_send, stat_recv, out_sem, hop_sem):
    batch, rows, columns, frames, classes = teacher.shape
    tokens, width = feats.shape
    ta, ha, wa = (lax.axis_index(axis) for axis in AXES)
    per_row = columns * frames
    slots = columns + 2
    sides = slots * frames
    outs = batch * per_row
    edges = planar.shape[2] - outs
    bits = n.bit_length() - 1
    owned = final.shape[0]
    has_left, has_right = wa > 0, wa < n - 1

    barrier = pltpu.get_barrier_semaphore()

    def greet(device):
        pl.semaphore_signal(barrier, inc=1, device_id=device, device_id_type=MESH)

    greet({"ta": 1 - ta})
    greet({"ha": 1 - ha})

    @pl.when(has_left)
    def _():
        greet({"wa": wa - 1})

    @pl.when(has_right)
    def _():
        greet({"wa": wa + 1})

    staged = logits.at[pl.ds(0, classes)]
    head_load = pltpu.make_async_copy(weight, staged, load_sem.at[0])
    head_load.start()
    fchunks = feat_sem.shape[0]
    chunk = tokens // fchunks

    def feat_rows(i):
        return pl.ds(pl.multiple_of(i * chunk, 16), chunk)

    def feat_load(i):
        return pltpu.make_async_copy(feats.at[feat_rows(i)], features.at[feat_rows(i)], feat_sem.at[i])

    @pl.loop(0, fchunks)
    def _(i):
        feat_load(i).start()

    cell_load = pltpu.make_async_copy(teacher, cells.at[:, pl.ds(0, rows), pl.ds(0, columns)], load_sem.at[1])
    cell_load.start()
    mine = (ta * 2 + ha) * n + wa
    first_row = mine * owned
    lane_block = pl.ds(pl.multiple_of(first_row // LANES * LANES, LANES), LANES)
    own_load = pltpu.make_async_copy(weight.at[:, lane_block], own_rows, load_sem.at[2])
    own_load.start()

    sends = (has_right, has_left)
    gets = (has_left, has_right)

    base = lax.rem(wa * columns + WV - WW // 2, WV)

    def clip_at(col):
        at = col + base
        return jnp.where(at < 0, -1, jnp.where(at >= WV, 1, 0))

    grid_wide = columns * n
    out = lax.broadcasted_iota(jnp.int32, pool.shape, 0)
    src = lax.broadcasted_iota(jnp.int32, pool.shape, 1)
    is_edge = out >= outs
    edge_at = out - outs
    main_batch = (out >= per_row).astype(jnp.int32)
    edge_batch = (edge_at >= columns).astype(jnp.int32)
    out_batch = jnp.where(is_edge, edge_batch, main_batch)
    main_in = out - main_batch * per_row
    out_col = jnp.where(is_edge, edge_at - edge_batch * columns, main_in // frames)
    out_frame = lax.rem(main_in, frames)
    src_batch = (src >= sides).astype(jnp.int32)
    src_in = src - src_batch * sides
    src_slot = src_in // frames
    src_frame = lax.rem(src_in, frames)
    src_col = jnp.where(src_slot == columns, -1, jnp.where(src_slot == columns + 1, columns, src_slot))
    edge_frame = jnp.where(ta == 0, frames - 1, 0)
    src_at = src_col + wa * columns
    away = jnp.where(is_edge, src_frame - edge_frame, src_frame - out_frame)
    reach = jnp.where(is_edge, 0, 1)
    taken = (
        (out_batch == src_batch) & (out_col < columns) & (jnp.abs(out_col - src_col) <= 1) & (jnp.abs(away) <= reach)
        & (src_at >= 0) & (src_at < grid_wide) & (clip_at(out_col) == clip_at(src_col))
    )
    pool[...] = jnp.where(taken, 1.0, 0.0).astype(jnp.bfloat16)
    cell = lax.broadcasted_iota(jnp.int32, inverse.shape, 0)
    col, frame = cell // frames, lax.rem(cell, frames)
    at = col + wa * columns
    left_ok = (at > 0) & (clip_at(col - 1) == clip_at(col))
    right_ok = (at < grid_wide - 1) & (clip_at(col + 1) == clip_at(col))
    frame_at = frame + ta * frames
    frame_edge = (frame_at == 0) | (frame_at == 2 * frames - 1)
    cols = 1.0 + jnp.where(left_ok, 1.0, 0.0) + jnp.where(right_ok, 1.0, 0.0)
    inverse[...] = EXP2_SCALE / (cols * jnp.where(frame_edge, 2.0, 3.0))

    for side in (0, 1):
        @pl.when(jnp.logical_not(gets[side]))
        def _():
            cells[:, :, columns + side] = jnp.zeros((batch, rows + 1, frames, classes), cells.dtype)

    planar[0] = jnp.zeros(planar.shape[1:], jnp.float32)

    padded = head.shape[0]
    blocks = padded // LANES
    head_load.wait()

    @pl.loop(0, blocks)
    def _(i):
        at = pl.ds(pl.multiple_of(i * LANES, LANES), LANES)
        class_at = lax.broadcasted_iota(jnp.int32, (LANES, 1), 0) + i * LANES
        head[at] = jnp.where(class_at < classes, logits[at], 0.0).astype(jnp.bfloat16)

    own_load.wait()
    own_turned[...] = own_rows[...].T

    pl.semaphore_wait(barrier, 2 + has_left.astype(jnp.int32) + has_right.astype(jnp.int32))

    col_chunks = col_send.shape[1]
    span = rows // col_chunks

    def col_copy(side, q):
        start = jnp.where(ha == 0, q * span, rows - (q + 1) * span)
        at = pl.ds(start, span)
        return pltpu.make_async_remote_copy(
            src_ref=teacher.at[:, at, columns - 1 if side == 0 else 0], dst_ref=cells.at[:, at, columns + side],
            send_sem=col_send.at[side, q], recv_sem=col_recv.at[side, q],
            device_id={"wa": wa + 1 if side == 0 else wa - 1}, device_id_type=MESH)

    facing = jnp.where(ha == 0, rows - 1, 0)

    def row_copy():
        return pltpu.make_async_remote_copy(
            src_ref=teacher.at[:, facing], dst_ref=cells.at[:, rows, pl.ds(0, columns)], send_sem=row_send.at[2], recv_sem=row_recv.at[2],
            device_id={"ha": 1 - ha}, device_id_type=MESH)

    def corner_copy(side):
        return pltpu.make_async_remote_copy(
            src_ref=teacher.at[:, facing, columns - 1 if side == 0 else 0], dst_ref=cells.at[:, rows, columns + side],
            send_sem=row_send.at[side], recv_sem=row_recv.at[side],
            device_id={"ha": 1 - ha, "wa": wa + 1 if side == 0 else wa - 1}, device_id_type=MESH)


    def start_columns(q):
        for side in (0, 1):
            @pl.when(sends[side])
            def _():
                col_copy(side, q).start()

    start_columns(0)
    start_columns(1)
    row_copy().start()

    def tell(r):
        far = 1 << r

        @pl.when(wa >= far)
        def _():
            pl.semaphore_signal(hop_sem.at[r], inc=1, device_id={"wa": wa - far}, device_id_type=MESH)

        @pl.when(wa + far < n)
        def _():
            pl.semaphore_signal(hop_sem.at[r], inc=1, device_id={"wa": wa + far}, device_id_type=MESH)

    def hear(r):
        far = 1 << r
        pl.semaphore_wait(hop_sem.at[r], (wa >= far).astype(jnp.int32) + (wa + far < n).astype(jnp.int32))

    tell(0)

    lane_at = lax.broadcasted_iota(jnp.int32, (GROUP, LANES), 1)
    real = lane_at < classes - (blocks - 1) * LANES

    def lanes(j):
        return pl.ds(j * LANES, LANES)

    def fold(values, op):
        values = list(values)
        while len(values) > 1:
            values = [op(*values[i : i + 2]) if i + 1 < len(values) else values[i] for i in range(0, len(values), 2)]
        return values[0]

    def masked(values):
        return values[:-1] + [jnp.where(real, values[-1], LOW)]

    @pl.loop(0, fchunks)
    def _(i):
        feat_load(i).wait()
        for q in range(2, col_chunks):
            @pl.when(i == min(PACE[min(q, len(PACE) - 1)], fchunks - 1))
            def _():
                start_columns(q)

        logits[feat_rows(i)] = lax.dot_general(features[feat_rows(i)], head[...], (((1,), (1,)), ((), ())), preferred_element_type=jnp.float32)

        @pl.loop(0, chunk // GROUP, unroll=7)
        def _(g):
            at = pl.ds(pl.multiple_of(i * chunk + g * GROUP, GROUP), GROUP)
            top = jnp.max(fold(masked([logits[at, lanes(j)] for j in range(blocks)]), jnp.maximum), -1, keepdims=True)
            peak[pl.ds(pl.multiple_of(g * GROUP, GROUP), GROUP)] = jnp.broadcast_to(top * EXP2_SCALE, (GROUP, LANES))

        @pl.loop(0, chunk // GROUP, unroll=7)
        def _(g):
            at = pl.ds(pl.multiple_of(i * chunk + g * GROUP, GROUP), GROUP)
            high = peak[pl.ds(pl.multiple_of(g * GROUP, GROUP), GROUP)]
            powers = [jnp.exp2(value * EXP2_SCALE - high) for value in masked([logits[at, lanes(j)] for j in range(blocks)])]
            norm = jnp.sum(fold(powers, jnp.add), -1, keepdims=True)
            shift[at] = high + jnp.log2(norm)

        for r in range(bits):
            @pl.when(i == r)
            def _():
                hear(r)
                if r == 0:
                    for side in (0, 1):
                        @pl.when(sends[side])
                        def _():
                            corner_copy(side).start()
                if r + 1 < bits:
                    tell(r + 1)

    cell_load.wait()
    total[...] = jnp.zeros_like(total)

    def row_of(k):
        return jnp.where(k > rows, rows, jnp.where(ha == 0, k - 1, rows - k))

    def edge_copy(k):
        return pltpu.make_async_remote_copy(
            src_ref=planar.at[lax.rem(k, RING), :, pl.ds(outs, edges)], dst_ref=partner.at[k],
            send_sem=edge_send.at[lax.rem(k, RING)], recv_sem=edge_recv.at[k], device_id={"ta": 1 - ta}, device_id_type=MESH)

    @pl.loop(1, rows + 2 + LAG)
    def _(it):
        @pl.when(it <= rows + 1)
        def _():
            @pl.when((it <= rows) & (lax.rem(it - 1, span) == 0))
            def _():
                for side in (0, 1):
                    @pl.when(gets[side])
                    def _():
                        col_copy(side, (it - 1) // span).wait_recv()

            @pl.when(it == rows + 1)
            def _():
                row_copy().wait_recv()
                for side in (0, 1):
                    @pl.when(gets[side])
                    def _():
                        corner_copy(side).wait_recv()

            @pl.when(it > RING)
            def _():
                edge_copy(it - RING).wait_send()

            here = cells[:, row_of(it)].reshape(batch * sides, classes)
            sums = jnp.dot(pool[...], here, preferred_element_type=jnp.float32)
            for j in range(blocks):
                wide = min(LANES, classes - j * LANES)
                planar[lax.rem(it, RING), j, :, pl.ds(0, wide)] = sums[:, j * LANES : j * LANES + wide]
            edge_copy(it).start()

        @pl.when(it > LAG)
        def _():
            edge_copy(it - LAG).wait_recv()
            slot = lax.rem(it - LAG, RING)
            at = pl.ds(jnp.where(ta == 0, frames - 1, 0), batch * columns, stride=frames)
            for j in range(blocks):
                planar[slot, j, at] += partner[it - LAG, j, pl.ds(0, batch * columns)]

        @pl.when(it > LAG + 1)
        def _():
            k = it - LAG - 1
            row = row_of(k)
            row_at = row + ha * rows
            row_scale = jnp.where((row_at == 0) | (row_at == 2 * rows - 1), 1.0 / 2.0, 1.0 / 3.0)
            before, now, after = (lax.rem(k + RING - 1, RING), lax.rem(k, RING), lax.rem(k + 1, RING))

            for b in range(batch):
                @pl.loop(0, per_row // GROUP, unroll=7)
                def _(g):
                    sl = pl.ds(pl.multiple_of(b * per_row + g * GROUP, GROUP), GROUP)
                    at = pl.ds(pl.multiple_of(b * (rows * per_row) + row * per_row + g * GROUP, GROUP), GROUP)
                    scale = inverse[pl.ds(pl.multiple_of(g * GROUP, GROUP), GROUP)] * row_scale
                    teach = masked([(planar[before, j, sl] + planar[now, j, sl] + planar[after, j, sl]) * scale for j in range(blocks)])
                    top = jnp.max(fold(teach, jnp.maximum), -1, keepdims=True)
                    teach = [value - top for value in teach]
                    powers = [jnp.exp2(value) for value in teach]
                    norm = jnp.sum(fold(powers, jnp.add), -1, keepdims=True)
                    learn = [value * EXP2_SCALE - shift[at] for value in masked([logits[at, lanes(j)] for j in range(blocks)])]
                    cross = jnp.sum(fold([power * (t - l) for power, t, l in zip(powers, teach, learn)], jnp.add), -1, keepdims=True)
                    total[...] += cross / norm - jnp.log2(norm)
                    weigh = 2.0 / norm
                    for j in range(blocks):
                        slope = jnp.exp2(learn[j] + 1.0) - powers[j] * weigh
                        slopes[at, lanes(j)] = slope.astype(jnp.bfloat16)

    @pl.loop(rows + 2 - RING, rows + 2)
    def _(k):
        edge_copy(k).wait_send()

    far_count = n // 2
    far, low = wa // 2, lax.rem(wa, 2)
    chunks = padded // HEAD_CHUNK
    halvings = 3

    def order(j):
        return (0, 1, 2) if j % 2 == 0 else (0, 2, 1)

    def partner_of(d):
        return ({"ta": 1 - ta}, {"ha": 1 - ha}, {"wa": far * 2 + 1 - low})[d]

    def region(j, s, other):
        seq = order(j)
        index = [slice(None)] * 3
        for d in seq[:s]:
            index[d] = (ta, ha, low)[d]
        own = (ta, ha, low)[seq[s]]
        index[seq[s]] = 1 - own if other else own
        return (j, index[0], index[1], slice(None), index[2])

    def landing(j, s):
        return landed[s].at[j] if s != 1 else landed[1 if j % 2 == 0 else 4].at[j // 2]

    def red_copy(j, s):
        return pltpu.make_async_remote_copy(
            src_ref=part.at[region(j, s, True)], dst_ref=landing(j, s), send_sem=red_send.at[j, s], recv_sem=red_recv.at[j, s],
            device_id=partner_of(order(j)[s]), device_id_type=MESH)

    def far_copy(j, k):
        to = lax.rem(far + k, far_count)
        return pltpu.make_async_remote_copy(
            src_ref=part.at[j, ta, ha, to, low], dst_ref=landed[halvings].at[j, k], send_sem=far_send.at[j, k], recv_sem=far_recv.at[j, k],
            device_id={"wa": to * 2 + low}, device_id_type=MESH)

    def head_grad(j, first):
        half = width // 2
        h = 1 - ta if first else ta
        grad = lax.dot_general(slopes[:, pl.ds(j * HEAD_CHUNK, HEAD_CHUNK)], features[:, pl.ds(pl.multiple_of(h * half, half), half)],
                               (((0,), (0,)), ((), ())), preferred_element_type=jnp.float32)
        part[j, h] = grad.astype(part.dtype).T.reshape(part.shape[2:])
        if first:
            red_copy(j, 0).start()

    def advance(j, s):
        if s < halvings:
            red_copy(j, s).wait_recv()
            part[region(j, s, False)] = (part[region(j, s, False)].astype(jnp.float32) + landing(j, s)[...].astype(jnp.float32)).astype(part.dtype)
            if s + 1 < halvings:
                red_copy(j, s + 1).start()
            else:
                @pl.loop(1, far_count)
                def _(k):
                    far_copy(j, k).start()
        else:
            columns_at = pl.ds(j * HEAD_CHUNK, HEAD_CHUNK)
            final[:, columns_at] = part[j, ta, ha, far, low].astype(jnp.float32)

            @pl.loop(1, far_count)
            def _(k):
                far_copy(j, k).wait_recv()
                final[:, columns_at] += landed[halvings][j, k].astype(jnp.float32)

    def out_copy(i):
        return pltpu.make_async_copy(features.at[feat_rows(i)], fgrad.at[feat_rows(i)], out_sem.at[i])

    def feature_grad(i):
        grad = jnp.dot(slopes[feat_rows(i)], head[...], preferred_element_type=jnp.float32)
        features[feat_rows(i)] = grad.astype(features.dtype)
        out_copy(i).start()

    begin = [(4.4, 2.5), (8.6, 2.6), (11.6, 2.6), (15.0, 2.4)]
    events = sorted((base + more * j, s, j) for s, (base, more) in enumerate(begin) for j in range(chunks))
    clock = 0.0
    work = [(functools.partial(head_grad, j, first), 1.25) for j in range(chunks) for first in (True, False)]
    work += [(functools.partial(feature_grad, i), 1.2) for i in range(fchunks)]
    for op, cost in work:
        op()
        clock += cost
        while events and events[0][0] <= clock:
            _, s, j = events.pop(0)
            advance(j, s)
    for _, s, j in events:
        advance(j, s)

    grad = final[...]
    squares = jnp.sum(jnp.sum(grad * grad, axis=1, keepdims=True), axis=0, keepdims=True)
    spent = jnp.sum(total[...], axis=0, keepdims=True) * (sharpness_divisor * sharpness_divisor * math.log(2.0))
    lane = lax.broadcasted_iota(jnp.int32, stat.shape, 1)
    stat[...] = jnp.where(lane == 0, squares, jnp.where(lane == 1, spent, 0.0))

    def stat_copy(k):
        to = lax.rem(mine + k, 4 * n)
        return pltpu.make_async_remote_copy(
            src_ref=stat, dst_ref=stat_in.at[mine], send_sem=stat_send.at[k], recv_sem=stat_recv.at[k],
            device_id={"ta": to // (2 * n), "ha": lax.rem(to // n, 2), "wa": lax.rem(to, n)}, device_id_type=MESH)

    @pl.loop(1, 4 * n)
    def _(k):
        stat_copy(k).start()

    stat_in[mine] = stat[...]

    @pl.loop(1, 4 * n)
    def _(k):
        stat_copy(k).wait_recv()

    both = jnp.sum(stat_in[...], axis=0)
    norm = jnp.sqrt(both[0:1, 0:1])
    loss[...] = both[0:1, 1:2]
    clip = jnp.minimum(1.0, clip_norm / (norm + 1e-06))
    own = own_turned[pl.ds(pl.multiple_of(lax.rem(first_row, LANES), owned), owned)]
    new_weight[...] = own - learn_rate * clip * final[:, pl.ds(0, classes)]

    @pl.loop(1, 4 * n)
    def _(k):
        stat_copy(k).wait_send()

    for j in range(chunks):
        for s in range(halvings):
            red_copy(j, s).wait_send()

        @pl.loop(1, far_count)
        def _(k):
            far_copy(j, k).wait_send()

    @pl.loop(0, fchunks)
    def _(i):
        out_copy(i).wait()

    row_copy().wait_send()
    for side in (0, 1):
        @pl.when(sends[side])
        def _():
            corner_copy(side).wait_send()

            @pl.loop(0, col_chunks)
            def _(q):
                col_copy(side, q).wait_send()


def local(features, teacher, head_weight):
    features, teacher = (jnp.transpose(array, (0, 2, 3, 1, 4)) for array in (features, teacher))
    batch, rows, columns, frames, width = features.shape
    classes = teacher.shape[-1]
    tokens = batch * rows * columns * frames
    n = lax.axis_size("wa")
    bits = n.bit_length() - 1
    devices = 4 * n
    owned = width // devices
    padded = -(-classes // HEAD_CHUNK) * HEAD_CHUNK
    chunks = padded // HEAD_CHUNK
    outs = batch * columns * frames
    edges = -(-(batch * columns) // 16) * 16
    fchunks = rows // 2
    col_chunks = rows // 2
    f32, bf16 = jnp.float32, jnp.bfloat16
    dma = pltpu.SemaphoreType.DMA
    any_space = pl.BlockSpec(memory_space=pl.ANY)
    vmem = pl.BlockSpec(memory_space=pltpu.VMEM)
    fgrad, loss, new_weight = pl.pallas_call(
        functools.partial(step_kernel, n),
        in_specs=[any_space] * 3,
        out_specs=[any_space, vmem, vmem],
        out_shape=[
            jax.ShapeDtypeStruct((tokens, width), features.dtype),
            jax.ShapeDtypeStruct((1, 1), f32),
            jax.ShapeDtypeStruct((owned, classes), f32),
        ],
        scratch_shapes=[
            pltpu.VMEM((batch, rows + 1, columns + 2, frames, classes), bf16),
            pltpu.VMEM((tokens, width), bf16),
            pltpu.VMEM((tokens, padded), f32),
            pltpu.VMEM((tokens, padded), bf16),
            pltpu.VMEM((padded, width), bf16),
            pltpu.VMEM((RING, padded // LANES, outs + edges, LANES), f32),
            pltpu.VMEM((rows + 2, padded // LANES, edges, LANES), f32),
            pltpu.VMEM((tokens // fchunks, LANES), f32),
            pltpu.VMEM((tokens, LANES), f32),
            pltpu.VMEM((outs + edges, batch * (columns + 2) * frames), bf16),
            pltpu.VMEM((columns * frames, 128), f32),
            pltpu.VMEM((chunks, 2, 2, n // 2, 2, owned, HEAD_CHUNK), bf16),
            pltpu.VMEM((owned, padded), f32),
            pltpu.VMEM((classes, LANES), f32),
            pltpu.VMEM((LANES, classes), f32),
            pltpu.VMEM((GROUP, 1), f32),
            pltpu.VMEM((8, 128), f32),
            pltpu.VMEM((devices, 8, 128), f32),
            [pltpu.VMEM(shape + (owned, HEAD_CHUNK), bf16) for shape in (
                (chunks, 2, n // 2, 2), ((chunks + 1) // 2, n // 2, 2), (chunks, n // 2), (chunks, n // 2), ((chunks + 1) // 2, 2, n // 2))],
            dma((3,)),
            dma((fchunks,)),
            dma((2, col_chunks)),
            dma((2, col_chunks)),
            dma((3,)),
            dma((3,)),
            dma((RING,)),
            dma((rows + 2,)),
            dma((chunks, 3)),
            dma((chunks, 3)),
            dma((chunks, n // 2)),
            dma((chunks, n // 2)),
            dma((devices,)),
            dma((devices,)),
            dma((fchunks,)),
            pltpu.SemaphoreType.REGULAR((bits,)),
        ],
        compiler_params=pltpu.CompilerParams(collective_id=0, has_side_effects=True, vmem_limit_bytes=63 * 1024 * 1024),
    )(teacher, features.reshape(tokens, width), head_weight.T)
    fgrad = jnp.transpose(fgrad.reshape(features.shape), (0, 3, 1, 2, 4))
    return fgrad, loss[0, 0], new_weight


def solution(mesh):
    assert mesh.shape["ta"] == 2 and mesh.shape["ha"] == 2
    placed = (P(None, "ta", "ha", "wa", None), P(None, "ta", "ha", "wa", None), P())
    return jax.shard_map(
        local,
        mesh=mesh,
        in_specs=placed,
        out_specs=(P(None, "ta", "ha", "wa", None), P(), P(AXES, None)),
        check_vma=False,
    )
```
